512 devices in a mesh: mesh: 64 (over y, z), band: 8 (over x, core).
Axes of the slice: x: 4, y: 4, z: 16, core: 2. Of those that a mesh axis runs over, the one named last changes fastest.
Arguments:
- state: bfloat16 [65536, 2048], P('mesh', 'band'), may hold values from -6 to 6
- prev_state: bfloat16 [65536, 2048], P('mesh', 'band'), may hold values from -6 to 6
- mass: float32 [65536], P('mesh'), may hold values from 0.1 to 1.9
- cell_nodes: int32 [256, 512], P('mesh'), may hold values from 0 to 1279, as said below
- cell_live: int32 [64], P('mesh'), may hold values from 1 to 4, 192 in all
- cell_scale: float32 [256], P('mesh'), may hold values from 0.5 to 2
- potential: float32 [256, 512], P('mesh'), may hold values from -6 to 6
- stiffness: bfloat16 [512, 512], replicated, may hold values from -0.25 to 0.25
- shape_values: bfloat16 [512, 512], replicated, may hold values from -0.25 to 0.25
- cell_proj: bfloat16 [256, 512, 128], P('mesh', 'band'), may hold values from -0.25 to 0.25
- cell_owner: int32 [256, 8], P('mesh'), may hold values from 0 to 63, as said below
- cell_slot: int32 [256, 8], P('mesh'), may hold values from 0 to 7, as said below
- coupling: float32 [512, 16], P('mesh'), may hold values from -6 to 6
- send_rows: int32 [64, 256], P('mesh'), may hold values from 0 to 1023, as said below
Outputs:
- filtered_one: bfloat16 [65536, 2048], P('mesh', 'band')
- filtered_two: bfloat16 [65536, 2048], P('mesh', 'band')
The draws below stay inside these ranges and needn't reach their ends.
Inputs may be any that keep to these rules, and one draw needn't show every extreme that they name: `cell_nodes`: the 512 entries of a cell are distinct; entries below 256 name the partition's ghost rows, the others its own node (entry minus 256); every entry value of a partition is named by some cell of it. `cell_live`: slots at or after this count are padding. `cell_owner`: the owners lie within two partitions of the cell's own; the 8 atoms of a cell are distinct. `cell_slot`: an atom's index among the 8 atoms of its owner. `send_rows`: each row holds distinct indices of the partition's own nodes; the last partition's row is not read.
All inputs are finite; a program needn't handle non-finite values. No bound on the sum of `cell_live` on one device may be relied on, other than what follows from the above.
Results may differ from the reference program's by a relative error of at most 0.0085.
Values may be sent and summed in bfloat16 or wider, within the bound.
No kernel may reach another device: no remote copies, remote signals or barrier semaphores. Data moves between devices by JAX's collectives and lax.ppermute only.
A program may use at most 64 MiB of HBM per device.

```python
import math
import jax
import jax.numpy as jnp
import numpy as np
from jax import lax

NPC = 512
QPC = 512
APC = 8
PPA = 16
PROJ = 128
CELL_DEV = 4
NODE_DEV = 1024
FACE = 256
ATOM_DEV = 8
NODES = 65536
CELLS = 256
ATOMS = 512
ORB = 2048
N_MESH = 64


def draw_cell_nodes(key, part):
    extended = FACE + NODE_DEV
    stride = (extended - NPC) // (CELL_DEV - 1)
    key_list = jax.random.split(key, N_MESH)
    shuffles = jax.vmap(lambda one_key: jax.random.permutation(one_key, extended))(key_list)
    positions = jnp.arange(CELL_DEV)[:, None] * stride + jnp.arange(NPC)[None, :]
    picked = shuffles[:, positions]
    return picked.reshape(N_MESH * CELL_DEV, NPC).astype(jnp.int32)


def atom_pairs(key):
    window = 5 * ATOM_DEV
    cell_keys = jax.random.split(jax.random.fold_in(key, 7), CELLS)
    ordering = jax.vmap(lambda one_key: jax.random.permutation(one_key, window))(cell_keys)
    partition = jnp.arange(CELLS) // CELL_DEV
    candidate = jnp.arange(window)
    owners = partition[:, None] + candidate[None, :] // ATOM_DEV - 2
    invalid = ((owners < 0) | (owners >= N_MESH)).astype(jnp.int32)
    scores = ordering + invalid * window
    chosen = jnp.argsort(scores, axis=1, stable=True)[:, :APC]
    picked_owner = jnp.take_along_axis(owners, chosen, axis=1)
    picked_slot = chosen % ATOM_DEV
    return (picked_owner.astype(jnp.int32), picked_slot.astype(jnp.int32))


def draw_cell_owner(key, part):
    return atom_pairs(key)[0]


def draw_cell_slot(key, part):
    return atom_pairs(key)[1]


def draw_send_rows(key, part):
    row_keys = jax.random.split(key, N_MESH)
    inner = jax.vmap(lambda one_key: jax.random.permutation(one_key, NODE_DEV - 2))(row_keys)[:, :FACE - 2] + 1
    ends = jnp.broadcast_to(jnp.array([0, NODE_DEV - 1], jnp.int32), (N_MESH, 2))
    joined = jnp.concatenate([ends, inner.astype(jnp.int32)], axis=1)
    mix_keys = jax.random.split(jax.random.fold_in(key, 3), N_MESH)
    mixed = jax.vmap(lambda one_key, row_values: jax.random.permutation(one_key, row_values))(mix_keys, joined)
    return mixed.astype(jnp.int32)


def level_of(rng, extent, cuts, smallest, high):
    loudness = 1.0
    for dim, blocks in cuts:
        steps = jax.random.uniform(jax.random.fold_in(jax.random.fold_in(rng, 6), dim), (blocks,), jnp.float32, smallest / len(cuts), high / len(cuts))
        loudness = loudness * jnp.repeat(jnp.exp(steps), extent[dim] // blocks).reshape((-1,) + (1,) * (len(extent) - 1 - dim))
    return loudness


def split_up(number_of, total, limit, slope):
    portions = [(1 << 20) // math.isqrt(grade ** slope) + 1 for grade in range(2, number_of + 1)]
    surplus, holding = total - limit - (number_of - 1), [1] * (number_of - 1)
    while surplus > 0:
        candidates = [i for i in range(number_of - 1) if holding[i] < limit]
        whole, left = sum([portions[i] for i in candidates]), surplus
        for i in candidates:
            addition = min(limit - holding[i], max(1, left * portions[i] // whole), surplus)
            holding[i] = holding[i] + addition
            surplus = surplus - addition
    return np.array([limit] + holding)


def ragged(stream_key, number_of, total, reach, slope):
    if number_of == 2:
        one = jax.random.randint(stream_key, (), max(1, total - reach), min(reach, total - 1) + 1)
        return jnp.stack([one, total - one])
    lengths = jnp.asarray(split_up(number_of, total, reach, slope), jnp.int32)
    pairs = (number_of - 1) // 2
    source_of, sink = lengths[1:1 + 2 * pairs:2], lengths[2:2 + 2 * pairs:2]
    slack = jnp.minimum(source_of - 1, reach - sink)
    moved = jax.random.randint(jax.random.fold_in(stream_key, 1), (pairs,), 0, 1 << 20) % (slack + 1)
    lengths = lengths.at[1:1 + 2 * pairs:2].set(source_of - moved).at[2:2 + 2 * pairs:2].set(sink + moved)
    return lengths[jax.random.permutation(jax.random.fold_in(stream_key, 2), number_of)]


def centred(stream_key, shape, deviation, limit, shards=(), held_as=jnp.bfloat16):
    values = jax.random.normal(stream_key, shape, jnp.float32) * deviation
    if len(shards) > 0:
        values = level_of(stream_key, shape, shards, -0.22, 0.18) * values
    return jnp.clip(values, min=-limit, max=limit).astype(held_as)


def setup_inputs(seed: int = 0) -> dict:
    arg_keys = jax.random.split(jax.random.key(seed), 15)
    state = centred(arg_keys[0], (NODES, ORB), 1.0, 6.0, ((0, 64), (1, 8)))
    prev_state = centred(arg_keys[1], (NODES, ORB), 1.0, 6.0, ((0, 64), (1, 8)))
    mass = jnp.clip(1.0 + 0.18 * jax.random.normal(arg_keys[2], (NODES,), jnp.float32), 0.1, 1.9)
    cell_nodes = draw_cell_nodes(jax.random.fold_in(arg_keys[14], 71), 0)
    cell_live = ragged(arg_keys[4], N_MESH, (3 * CELL_DEV * N_MESH) // 4, CELL_DEV, 1).astype(jnp.int32)
    cell_scale = jnp.clip(jnp.exp(math.log(2.0) - 1.3862944 * jax.random.uniform(arg_keys[5], (CELLS,), jnp.float32) ** level_of(arg_keys[5], (CELLS,), ((0, 64),), -0.2, 0.2)), 0.5, 2.0)
    potential = centred(arg_keys[6], (CELLS, QPC), 1.0, 6.0, ((0, 64),), jnp.float32)
    stiffness = centred(arg_keys[7], (NPC, NPC), NPC ** -0.5, 0.25)
    shape_values = centred(arg_keys[8], (QPC, NPC), NPC ** -0.5, 0.25)
    cell_proj = centred(arg_keys[9], (CELLS, NPC, PROJ), NPC ** -0.5, 0.25, ((0, 64), (1, 8)))
    cell_owner = draw_cell_owner(jax.random.fold_in(arg_keys[14], 71), 0)
    cell_slot = draw_cell_slot(jax.random.fold_in(arg_keys[14], 71), 0)
    coupling = centred(arg_keys[12], (ATOMS, PPA), 1.0, 6.0, ((0, 64),), jnp.float32)
    send_rows = draw_send_rows(jax.random.fold_in(arg_keys[14], 71), 0)
    return {"state": state, "prev_state": prev_state, "mass": mass, "cell_nodes": cell_nodes, "cell_live": cell_live, "cell_scale": cell_scale, "potential": potential, "stiffness": stiffness, "shape_values": shape_values, "cell_proj": cell_proj, "cell_owner": cell_owner, "cell_slot": cell_slot, "coupling": coupling, "send_rows": send_rows}


filter_scale = 0.6
filter_shift = 1.0


def widen(values):
    return values.astype(jnp.float32)


def cell_blocks(ghost_rows, own_rows, node_map, alive_mask):
    extended = jnp.concatenate([ghost_rows, own_rows], axis=0)
    return extended[node_map] * alive_mask[:, None, None]


def reference(state, prev_state, mass, cell_nodes, cell_live, cell_scale, potential, stiffness, shape_values, cell_proj, cell_owner, cell_slot, coupling, send_rows):
    orbitals = state.shape[1]
    atom_ids = (cell_owner * ATOM_DEV + cell_slot).reshape(-1).astype(jnp.int32)
    alive_all = (jnp.arange(CELL_DEV)[None, :] < cell_live[:, None]).astype(jnp.bfloat16)
    node_maps = cell_nodes.reshape(N_MESH, CELL_DEV, NPC)
    proj_blocks = cell_proj.reshape(N_MESH, CELL_DEV, NPC, PROJ)
    scale_blocks = cell_scale.reshape(N_MESH, CELL_DEV)
    potential_blocks = potential.reshape(N_MESH, CELL_DEV, QPC)
    highest = lax.Precision.HIGHEST

    def apply(field):
        scaled = (mass[:, None] * field).astype(jnp.bfloat16).reshape(N_MESH, NODE_DEV, orbitals)
        outgoing = jnp.take_along_axis(scaled, send_rows[:, :, None], axis=1)
        ghosts = jnp.concatenate([jnp.zeros_like(outgoing[:1]), outgoing[:-1]], axis=0)

        def partials(inputs):
            ghost_rows, own_rows, node_map, alive_mask, cell_block = inputs
            nodal = cell_blocks(ghost_rows, own_rows, node_map, alive_mask)
            return jnp.einsum("cnk,cno->cko", widen(cell_block), widen(nodal), precision=highest)

        coefficients = lax.map(partials, (ghosts, scaled, node_maps, alive_all, proj_blocks))
        atom_sums = jax.ops.segment_sum(coefficients.reshape(CELLS * APC, PPA, orbitals), atom_ids, num_segments=ATOMS)
        atom_values = (coupling[:, :, None] * atom_sums).astype(jnp.bfloat16)
        coupled_all = atom_values[atom_ids].reshape(N_MESH, CELL_DEV, PROJ, orbitals)

        def cell_output(inputs):
            ghost_rows, own_rows, node_map, alive_mask, cell_block, cell_size, cell_potential, cell_coupled = inputs
            nodal = widen(cell_blocks(ghost_rows, own_rows, node_map, alive_mask))
            stiff_part = jnp.einsum("ij,cjo->cio", widen(stiffness), nodal, precision=highest)
            at_points = jnp.einsum("qj,cjo->cqo", widen(shape_values), nodal, precision=highest)
            rounded = (cell_potential[:, :, None] * at_points).astype(jnp.bfloat16)
            weighted = widen(lax.optimization_barrier(rounded))
            potential_part = jnp.einsum("qi,cqo->cio", widen(shape_values), weighted, precision=highest)
            proj_part = jnp.einsum("cnk,cko->cno", widen(cell_block), widen(cell_coupled), precision=highest)
            totals = (0.5 * cell_size[:, None, None] * stiff_part + potential_part + proj_part) * widen(alive_mask)[:, None, None]
            assembled = jnp.zeros((FACE + NODE_DEV, orbitals), jnp.float32)
            assembled = assembled.at[node_map.reshape(-1)].add(totals.reshape(-1, orbitals))
            return assembled[FACE:], assembled[:FACE]

        owned, ghost_sums = lax.map(cell_output, (ghosts, scaled, node_maps, alive_all, proj_blocks, scale_blocks, potential_blocks, coupled_all))
        incoming = jnp.concatenate([ghost_sums[1:], jnp.zeros_like(ghost_sums[:1])], axis=0)
        owned = jax.vmap(lambda node_rows, row_index, extra_rows: node_rows.at[row_index].add(extra_rows))(owned, send_rows, incoming)
        return mass[:, None] * owned.reshape(NODES, orbitals)

    current = widen(state)
    earlier = widen(prev_state)
    first = (filter_scale * (apply(current) - filter_shift * current) - earlier).astype(jnp.bfloat16)
    first_wide = widen(first)
    second = (filter_scale * (apply(first_wide) - filter_shift * first_wide) - current).astype(jnp.bfloat16)
    return first, second
```

```python
import jax
import jax.numpy as jnp
from jax import lax
from jax.experimental import pallas as pl
from jax.experimental.pallas import tpu as pltpu
from jax.sharding import PartitionSpec as P


APC = 8
F32 = jnp.float32
BF16 = jnp.bfloat16
LANES = 128

filter_scale = 0.6
filter_shift = 1.0

VMEM = pl.BlockSpec(memory_space=pltpu.VMEM)
SMEM = pl.BlockSpec(memory_space=pltpu.SMEM)


def from_behind(block, axis, distance):
    devices = range(lax.axis_size(axis))
    route = [(i - distance, i) for i in devices if i - distance in devices]
    return lax.ppermute(block, axis, route)


def dot(a, b):
    return jnp.dot(a, b, preferred_element_type=F32)


def column(row):
    n = row.shape[1]
    parts = [
        jnp.transpose(jnp.broadcast_to(row[:, i : i + LANES], (LANES, LANES)))
        for i in range(0, n, LANES)
    ]
    return jnp.concatenate(parts, axis=0)


def widen(col, width):
    return jnp.concatenate([col] * (width // LANES), axis=1)


def hot_rows(row, width):
    col = column(row.astype(F32)).astype(jnp.int32)
    lane = lax.broadcasted_iota(jnp.int32, col.shape, 1)
    parts = [(col == lane + i).astype(F32).astype(BF16) for i in range(0, width, LANES)]
    return jnp.concatenate(parts, axis=1)


def hot_columns(row, height):
    n = row.shape[1]
    line = lax.broadcasted_iota(jnp.int32, (height, n), 0)
    return (line == row).astype(F32).astype(BF16)


def start_kernel(state, mass, send, scaled, outgoing):
    m = widen(column(mass[...]), state.shape[1])
    scaled[...] = (m * state[...].astype(F32)).astype(BF16)
    face = send.shape[1]
    outgoing[0:face, :] = dot(hot_rows(send[...], state.shape[0]), scaled[...]).astype(BF16)
    high = mass[...].astype(BF16)
    rest = mass[...] - high.astype(F32)
    middle = rest.astype(BF16)
    low = rest - middle.astype(F32)
    line = lax.broadcasted_iota(jnp.int32, (16, mass.shape[1]), 0)
    split = jnp.where(
        line == 0,
        high.astype(F32),
        jnp.where(line == 1, middle.astype(F32), jnp.where(line == 2, low, 0.0)),
    ).astype(BF16)
    outgoing[face : face + 16, :] = dot(split, hot_columns(send[...], state.shape[0])).astype(BF16)


def setup_kernel(nodes, potential, stiffness, shape_values, live, scale, pick, place, operator):
    c = pl.program_id(0)
    row = nodes[pl.ds(c, 1), :]
    extended = place.shape[1]
    pick[0] = hot_rows(row, extended)
    place[0] = hot_columns(row, extended)
    points = column(potential[pl.ds(c, 1), :])
    values = shape_values[...].astype(F32)
    weighted = (widen(points, values.shape[1]) * values).astype(BF16)
    local = dot(jnp.transpose(shape_values[...]), weighted)
    alive = jnp.where(c < live[0], 1.0, 0.0)
    operator[0] = (alive * (0.5 * scale[c] * stiffness[...].astype(F32) + local)).astype(BF16)


def table_kernel(
    projectors, pick, owner, slot, live, partition, ghost, scaled, table, sums, wide, field
):
    cells = pick.shape[0]
    face = scaled.shape[0] // 4
    wide[...] = jnp.zeros_like(wide)
    field[0:face, :] = ghost[0:face, :]
    field[face:, :] = scaled[...]
    for c in range(cells):
        block = projectors[:, c].reshape(pick.shape[1], projectors.shape[3])
        at_nodes = dot(jnp.transpose(block), pick[c])
        at_nodes = at_nodes * jnp.where(c < live[0], 1.0, 0.0)
        for j in range(APC):
            target = (owner[c, j] - partition[0] + 2) * APC + slot[c, j]
            rows = pl.ds(pl.multiple_of(target * 16, 16), 16)
            wide[rows, :] = wide[rows, :] + at_nodes[16 * j : 16 * j + 16, :]
    table[...] = wide[...].astype(BF16)
    sums[...] = dot(table[...], field[...]).astype(BF16)


def turn_kernel(table, turned):
    turned[...] = jnp.transpose(table[...])


def local_kernel(pick, place, operator, ghost, scaled, out, field):
    face = scaled.shape[0] // 4

    @pl.when(pl.program_id(0) == 0)
    def _():
        field[0:face, :] = ghost[0:face, :]
        field[face:, :] = scaled[...]
        out[...] = jnp.zeros_like(out)

    cell = dot(pick[0], field[...]).astype(BF16)
    term = dot(operator[0], cell).astype(BF16)
    out[...] += dot(place[0], term)


def apply_out(turned, v0, v1, v2, v3, v4, local):
    values = jnp.concatenate([v0[...], v1[...], v2[...], v3[...], v4[...]], axis=0)
    return local[...] + dot(turned[...], values)


def middle_kernel(
    turned, v0, v1, v2, v3, v4, local, state, prev, mass, send, returned, own, edge
):
    face = send.shape[1]
    total = apply_out(turned, v0, v1, v2, v3, v4, local)
    returned[...] = total[0:face, :].astype(BF16)
    own[...] = total[face:, :]
    m = widen(column(mass[...]), state.shape[1])
    current = state[...].astype(F32)
    partial = filter_scale * (m * own[...] - filter_shift * current) - prev[...].astype(F32)
    edge[...] = dot(hot_rows(send[...], state.shape[0]), (m * partial).astype(BF16)).astype(BF16)


def next_kernel(
    own, received, edge, returned, ghost, state, prev, mass, send, table,
    first, scaled, ghost_next, sums, field,
):
    face = send.shape[1]
    m = widen(column(mass[...]), state.shape[1])
    owned = own[...] + dot(hot_columns(send[...], state.shape[0]), received[...])
    current = state[...].astype(F32)
    one = filter_scale * (m * owned - filter_shift * current) - prev[...].astype(F32)
    first[...] = one.astype(BF16)
    scaled[...] = (m * first[...].astype(F32)).astype(BF16)
    split = ghost[face : face + 16, :].astype(F32)
    g = widen(column(split[0:1, :] + split[1:2, :] + split[2:3, :]), state.shape[1])
    ghost_next[...] = (
        edge[...].astype(F32) + (filter_scale * g * g) * returned[...].astype(F32)
    ).astype(BF16)
    field[0:face, :] = ghost_next[...]
    field[face:, :] = scaled[...]
    sums[...] = dot(table[...], field[...]).astype(BF16)


def end_kernel(turned, v0, v1, v2, v3, v4, local, returned, own):
    face = returned.shape[0]
    total = apply_out(turned, v0, v1, v2, v3, v4, local)
    returned[...] = total[0:face, :].astype(BF16)
    own[...] = total[face:, :]


def last_kernel(own, received, state, first, mass, send, second):
    m = widen(column(mass[...]), state.shape[1])
    owned = own[...] + dot(hot_columns(send[...], state.shape[0]), received[...])
    two = filter_scale * (m * owned - filter_shift * first[...].astype(F32))
    second[...] = (two - state[...].astype(F32)).astype(BF16)


def call(kernel, outs, args, specs=None, scratch=(), **more):
    return pl.pallas_call(
        kernel,
        out_shape=[jax.ShapeDtypeStruct(s, d) for s, d in outs],
        in_specs=specs or [VMEM] * len(args),
        out_specs=more.pop("out_specs", [VMEM] * len(outs)),
        scratch_shapes=list(scratch),
        **more,
    )(*args)


def shards(
    state,
    prev_state,
    mass,
    cell_nodes,
    cell_live,
    cell_scale,
    potential,
    stiffness,
    shape_values,
    cell_proj,
    cell_owner,
    cell_slot,
    coupling,
    send_rows,
):
    own_rows, orbitals = state.shape
    cells, per_cell = cell_nodes.shape
    atoms, per_atom = coupling.shape
    face = send_rows.shape[1]
    extended = own_rows + face
    block = atoms * per_atom
    window = 5 * block
    mass_row = mass.reshape(1, own_rows)
    partition = lax.axis_index("mesh").astype(jnp.int32).reshape(1)

    scaled, outgoing = call(
        start_kernel,
        [((own_rows, orbitals), BF16), ((face + 16, orbitals), BF16)],
        (state, mass_row, send_rows),
    )
    ghost = from_behind(outgoing, "mesh", 1)

    pick, place, operator = call(
        setup_kernel,
        [
            ((cells, per_cell, extended), BF16),
            ((cells, extended, per_cell), BF16),
            ((cells, per_cell, per_cell), BF16),
        ],
        (cell_nodes, potential, stiffness, shape_values, cell_live, cell_scale),
        specs=[VMEM, VMEM, VMEM, VMEM, SMEM, SMEM],
        grid=(cells,),
        out_specs=[
            pl.BlockSpec((1, per_cell, extended), lambda c: (c, 0, 0)),
            pl.BlockSpec((1, extended, per_cell), lambda c: (c, 0, 0)),
            pl.BlockSpec((1, per_cell, per_cell), lambda c: (c, 0, 0)),
        ],
    )
    projectors = lax.all_gather(cell_proj, "band", axis=0, tiled=False)

    table, sums = call(
        table_kernel,
        [((window, extended), BF16), ((window, orbitals), BF16)],
        (projectors, pick, cell_owner, cell_slot, cell_live, partition, ghost, scaled),
        specs=[VMEM, VMEM, SMEM, SMEM, SMEM, SMEM, VMEM, VMEM],
        scratch=[pltpu.VMEM((window, extended), F32), pltpu.VMEM((extended, orbitals), BF16)],
    )
    (turned,) = call(turn_kernel, [((extended, window), BF16)], (table,))

    def atom_values(sums):
        parts = sums.reshape(5, atoms, per_atom, orbitals)
        total = parts[2].astype(F32)
        for offset in (1, 2, -1, -2):
            total = total + from_behind(parts[offset + 2], "mesh", offset).astype(F32)
        mine = (coupling[:, :, None] * total).astype(BF16)
        blocks = {0: mine}
        for offset in (1, 2, -1, -2):
            blocks[offset] = from_behind(mine, "mesh", -offset)
        return [blocks[o].reshape(block, orbitals) for o in (-2, -1, 0, 1, 2)]

    def local_part(ghost, scaled):
        return call(
            local_kernel,
            [((extended, orbitals), F32)],
            (pick, place, operator, ghost, scaled),
            specs=[
                pl.BlockSpec((1, per_cell, extended), lambda c: (c, 0, 0)),
                pl.BlockSpec((1, extended, per_cell), lambda c: (c, 0, 0)),
                pl.BlockSpec((1, per_cell, per_cell), lambda c: (c, 0, 0)),
                VMEM,
                VMEM,
            ],
            scratch=[pltpu.VMEM((extended, orbitals), BF16)],
            grid=(cells,),
            out_specs=[VMEM],
        )[0]

    nodal = ((own_rows, orbitals), BF16)
    shared = ((face, orbitals), BF16)
    own_wide = ((own_rows, orbitals), F32)

    local = local_part(ghost, scaled)
    values = atom_values(sums)
    returned, own, edge = call(
        middle_kernel,
        [shared, own_wide, shared],
        (turned, *values, local, state, prev_state, mass_row, send_rows),
    )
    received = from_behind(returned, "mesh", -1)
    edge_in = from_behind(edge, "mesh", 1)
    first, scaled_one, ghost_one, sums_one = call(
        next_kernel,
        [nodal, nodal, shared, ((window, orbitals), BF16)],
        (own, received, edge_in, returned, ghost, state, prev_state, mass_row, send_rows, table),
        scratch=[pltpu.VMEM((extended, orbitals), BF16)],
    )
    local_one = local_part(ghost_one, scaled_one)
    values_one = atom_values(sums_one)
    returned_one, own_one = call(
        end_kernel, [shared, own_wide], (turned, *values_one, local_one)
    )
    received_one = from_behind(returned_one, "mesh", -1)
    (second,) = call(
        last_kernel, [nodal], (own_one, received_one, state, first, mass_row, send_rows)
    )
    return (first, second)


def solution(mesh):
    placed = (
        P("mesh", "band"),
        P("mesh", "band"),
        P("mesh"),
        P("mesh", None),
        P("mesh"),
        P("mesh"),
        P("mesh", None),
        P(),
        P(),
        P("mesh", "band", None),
        P("mesh", None),
        P("mesh", None),
        P("mesh", None),
        P("mesh", None),
    )
    return jax.shard_map(
        shards,
        mesh=mesh,
        in_specs=placed,
        out_specs=(P("mesh", "band"), P("mesh", "band")),
        check_vma=False,
    )
```

```python
import jax
import jax.numpy as jnp
from jax import lax
from jax.experimental import pallas as pl
from jax.experimental.pallas import tpu as pltpu
from jax.sharding import PartitionSpec as P


APC = 8
F32 = jnp.float32
BF16 = jnp.bfloat16
LANES = 128

filter_scale = 0.6
filter_shift = 1.0

VMEM = pl.BlockSpec(memory_space=pltpu.VMEM)
SMEM = pl.BlockSpec(memory_space=pltpu.SMEM)


def from_behind(block, axis, distance):
    devices = range(lax.axis_size(axis))
    route = [(i - distance, i) for i in devices if i - distance in devices]
    return lax.ppermute(block, axis, route)


def dot(a, b):
    return jnp.dot(a, b, preferred_element_type=F32)


def column(row):
    n = row.shape[1]
    parts = [
        jnp.transpose(jnp.broadcast_to(row[:, i : i + LANES], (LANES, LANES)))
        for i in range(0, n, LANES)
    ]
    return jnp.concatenate(parts, axis=0)


def widen(col, width):
    return jnp.concatenate([col] * (width // LANES), axis=1)


def hot_rows(row, width):
    col = column(row.astype(F32)).astype(jnp.int32)
    lane = lax.broadcasted_iota(jnp.int32, col.shape, 1)
    parts = [(col == lane + i).astype(F32).astype(BF16) for i in range(0, width, LANES)]
    return jnp.concatenate(parts, axis=1)


def hot_columns(row, height):
    n = row.shape[1]
    line = lax.broadcasted_iota(jnp.int32, (height, n), 0)
    return (line == row).astype(F32).astype(BF16)


def start_kernel(state, mass, send, scaled, outgoing):
    m = widen(column(mass[...]), state.shape[1])
    scaled[...] = (m * state[...].astype(F32)).astype(BF16)
    face = send.shape[1]
    outgoing[0:face, :] = dot(hot_rows(send[...], state.shape[0]), scaled[...]).astype(BF16)
    high = mass[...].astype(BF16)
    rest = mass[...] - high.astype(F32)
    middle = rest.astype(BF16)
    low = rest - middle.astype(F32)
    line = lax.broadcasted_iota(jnp.int32, (16, mass.shape[1]), 0)
    split = jnp.where(
        line == 0,
        high.astype(F32),
        jnp.where(line == 1, middle.astype(F32), jnp.where(line == 2, low, 0.0)),
    ).astype(BF16)
    outgoing[face : face + 16, :] = dot(split, hot_columns(send[...], state.shape[0])).astype(BF16)


def hot_kernel(nodes, pick, place):
    cells, per_cell = nodes.shape
    extended = place.shape[0]
    for c in range(cells):
        row = nodes[c : c + 1, :]
        pick[c * per_cell : (c + 1) * per_cell, :] = hot_rows(row, extended)
        place[:, c * per_cell : (c + 1) * per_cell] = hot_columns(row, extended)


def operator_kernel(potential, stiffness, shape_values, live, scale, operator):
    values = shape_values[...].astype(F32)
    turned = jnp.transpose(shape_values[...])
    for c in range(potential.shape[0]):
        points = column(potential[c : c + 1, :])
        weighted = (widen(points, values.shape[1]) * values).astype(BF16)
        alive = jnp.where(c < live[0], 1.0, 0.0)
        local = 0.5 * scale[c] * stiffness[...].astype(F32) + dot(turned, weighted)
        operator[c] = (alive * local).astype(BF16)


def store_sums(table, field, outs):
    block = outs[0].shape[0]
    for i, out in enumerate(outs):
        out[...] = dot(table[i * block : (i + 1) * block, :], field[...]).astype(BF16)


def table_kernel(
    projectors, pick, owner, slot, live, partition, ghost, scaled,
    table, s0, s1, s2, s3, s4, wide, field,
):
    cells, per_atom = owner.shape[0], s0.shape[0] // APC
    per_cell = pick.shape[0] // cells
    face = scaled.shape[0] // 4
    wide[...] = jnp.zeros_like(wide)
    field[0:face, :] = ghost[0:face, :]
    field[face:, :] = scaled[...]
    for c in range(cells):
        shards_of = [projectors[i % 2, i // 2, c] for i in range(8)]
        block = jnp.concatenate(shards_of, axis=0)
        at_nodes = dot(jnp.transpose(block), pick[c * per_cell : (c + 1) * per_cell, :])
        at_nodes = at_nodes * jnp.where(c < live[0], 1.0, 0.0)
        for j in range(APC):
            target = (owner[c, j] - partition[0] + 2) * APC + slot[c, j]
            rows = pl.ds(pl.multiple_of(target * per_atom, per_atom), per_atom)
            wide[rows, :] = wide[rows, :] + at_nodes[per_atom * j : per_atom * (j + 1), :]
    table[...] = wide[...].astype(BF16)
    store_sums(table, field, (s0, s1, s2, s3, s4))


def turn_kernel(table, turned):
    turned[...] = jnp.transpose(table[...])


def gather_kernel(pick, operator, ghost, scaled, terms, field):
    face = scaled.shape[0] // 4
    cells, per_cell = operator.shape[0], operator.shape[1]
    field[0:face, :] = ghost[0:face, :]
    field[face:, :] = scaled[...]
    for c in range(cells):
        rows = slice(c * per_cell, (c + 1) * per_cell)
        cell = dot(pick[rows, :], field[...]).astype(BF16)
        terms[rows, :] = dot(operator[c], cell).astype(BF16)


def scatter_kernel(place, terms, out):
    out[...] = dot(place[...], terms[...])


def apply_out(turned, v0, v1, v2, v3, v4, local):
    values = jnp.concatenate([v0[...], v1[...], v2[...], v3[...], v4[...]], axis=0)
    return local[...] + dot(turned[...], values)


def middle_kernel(
    turned, v0, v1, v2, v3, v4, local, state, prev, mass, send, returned, own, edge
):
    face = send.shape[1]
    total = apply_out(turned, v0, v1, v2, v3, v4, local)
    returned[...] = total[0:face, :].astype(BF16)
    own[...] = total[face:, :]
    m = widen(column(mass[...]), state.shape[1])
    current = state[...].astype(F32)
    partial = filter_scale * (m * own[...] - filter_shift * current) - prev[...].astype(F32)
    edge[...] = dot(hot_rows(send[...], state.shape[0]), (m * partial).astype(BF16)).astype(BF16)


def next_kernel(
    own, received, edge, returned, ghost, state, prev, mass, send, table,
    first, scaled, ghost_next, s0, s1, s2, s3, s4, field,
):
    face = send.shape[1]
    m = widen(column(mass[...]), state.shape[1])
    owned = own[...] + dot(hot_columns(send[...], state.shape[0]), received[...])
    current = state[...].astype(F32)
    one = filter_scale * (m * owned - filter_shift * current) - prev[...].astype(F32)
    first[...] = one.astype(BF16)
    scaled[...] = (m * first[...].astype(F32)).astype(BF16)
    split = ghost[face : face + 16, :].astype(F32)
    g = widen(column(split[0:1, :] + split[1:2, :] + split[2:3, :]), state.shape[1])
    ghost_next[...] = (
        edge[...].astype(F32) + (filter_scale * g * g) * returned[...].astype(F32)
    ).astype(BF16)
    field[0:face, :] = ghost_next[...]
    field[face:, :] = scaled[...]
    store_sums(table, field, (s0, s1, s2, s3, s4))


def end_kernel(turned, v0, v1, v2, v3, v4, local, returned, own):
    face = returned.shape[0]
    total = apply_out(turned, v0, v1, v2, v3, v4, local)
    returned[...] = total[0:face, :].astype(BF16)
    own[...] = total[face:, :]


def last_kernel(own, received, state, first, mass, send, second):
    m = widen(column(mass[...]), state.shape[1])
    owned = own[...] + dot(hot_columns(send[...], state.shape[0]), received[...])
    two = filter_scale * (m * owned - filter_shift * first[...].astype(F32))
    second[...] = (two - state[...].astype(F32)).astype(BF16)


def call(kernel, outs, args, specs=None, scratch=(), mib=8):
    return pl.pallas_call(
        kernel,
        out_shape=[jax.ShapeDtypeStruct(shape, kind) for shape, kind in outs],
        in_specs=specs or [VMEM] * len(args),
        out_specs=[VMEM] * len(outs),
        scratch_shapes=list(scratch),
        compiler_params=pltpu.CompilerParams(vmem_limit_bytes=mib << 20),
    )(*args)


def shards(
    state,
    prev_state,
    mass,
    cell_nodes,
    cell_live,
    cell_scale,
    potential,
    stiffness,
    shape_values,
    cell_proj,
    cell_owner,
    cell_slot,
    coupling,
    send_rows,
):
    own_rows, orbitals = state.shape
    cells, per_cell = cell_nodes.shape
    atoms, per_atom = coupling.shape
    face = send_rows.shape[1]
    extended = own_rows + face
    block = atoms * per_atom
    window = 5 * block
    mass_row = mass.reshape(1, own_rows)
    partition = lax.axis_index("mesh").astype(jnp.int32).reshape(1)

    scaled, outgoing = call(
        start_kernel,
        [((own_rows, orbitals), BF16), ((face + 16, orbitals), BF16)],
        (state, mass_row, send_rows),
    )
    ghost = from_behind(outgoing, "mesh", 1)

    pick, place = call(
        hot_kernel,
        [((cells * per_cell, extended), BF16), ((extended, cells * per_cell), BF16)],
        (cell_nodes,),
    )
    (operator,) = call(
        operator_kernel,
        [((cells, per_cell, per_cell), BF16)],
        (potential, stiffness, shape_values, cell_live, cell_scale),
        specs=[VMEM, VMEM, VMEM, SMEM, SMEM],
    )
    projectors = cell_proj
    for groups in ([[0, 2], [4, 6], [1, 3], [5, 7]], [[0, 6], [2, 4], [1, 7], [3, 5]]):
        projectors = lax.all_gather(
            projectors, "band", axis=0, tiled=projectors is not cell_proj, axis_index_groups=groups
        )
    projectors = lax.all_gather(
        projectors, "band", axis=0, axis_index_groups=[[0, 1], [2, 3], [4, 5], [6, 7]]
    )

    part = ((block, orbitals), BF16)
    table, *sums = call(
        table_kernel,
        [((window, extended), BF16)] + [part] * 5,
        (projectors, pick, cell_owner, cell_slot, cell_live, partition, ghost, scaled),
        specs=[VMEM, VMEM, SMEM, SMEM, SMEM, SMEM, VMEM, VMEM],
        scratch=[pltpu.VMEM((window, extended), F32), pltpu.VMEM((extended, orbitals), BF16)],
    )
    (turned,) = call(turn_kernel, [((extended, window), BF16)], (table,))

    def atom_values(sums, terms):
        received = [from_behind(sums[o + 2], "mesh", o) for o in (1, 2, -1, -2)]
        received, terms = lax.optimization_barrier((received, terms))
        total = sums[2].astype(F32)
        for piece in received:
            total = total + piece.astype(F32)
        total = coupling[:, :, None] * total.reshape(atoms, per_atom, orbitals)
        mine = total.astype(BF16).reshape(block, orbitals)
        blocks = {0: mine}
        for offset in (1, 2, -1, -2):
            blocks[offset] = from_behind(mine, "mesh", -offset)
        (local,) = call(scatter_kernel, [((extended, orbitals), F32)], (place, terms))
        return [blocks[o] for o in (-2, -1, 0, 1, 2)], local

    def cell_terms(ghost, scaled):
        (terms,) = call(
            gather_kernel,
            [((cells * per_cell, orbitals), BF16)],
            (pick, operator, ghost, scaled),
            scratch=[pltpu.VMEM((extended, orbitals), BF16)],
        )
        return terms

    nodal = ((own_rows, orbitals), BF16)
    shared = ((face, orbitals), BF16)
    own_wide = ((own_rows, orbitals), F32)

    values, local = atom_values(sums, cell_terms(ghost, scaled))
    returned, own, edge = call(
        middle_kernel,
        [shared, own_wide, shared],
        (turned, *values, local, state, prev_state, mass_row, send_rows),
    )
    received = from_behind(returned, "mesh", -1)
    edge_in = from_behind(edge, "mesh", 1)
    first, scaled_one, ghost_one, *sums_one = call(
        next_kernel,
        [nodal, nodal, shared] + [part] * 5,
        (own, received, edge_in, returned, ghost, state, prev_state, mass_row, send_rows, table),
        scratch=[pltpu.VMEM((extended, orbitals), BF16)],
    )
    values_one, local_one = atom_values(sums_one, cell_terms(ghost_one, scaled_one))
    returned_one, own_one = call(
        end_kernel, [shared, own_wide], (turned, *values_one, local_one)
    )
    received_one = from_behind(returned_one, "mesh", -1)
    (second,) = call(
        last_kernel, [nodal], (own_one, received_one, state, first, mass_row, send_rows)
    )
    return (first, second)


def solution(mesh):
    placed = (
        P("mesh", "band"),
        P("mesh", "band"),
        P("mesh"),
        P("mesh", None),
        P("mesh"),
        P("mesh"),
        P("mesh", None),
        P(),
        P(),
        P("mesh", "band", None),
        P("mesh", None),
        P("mesh", None),
        P("mesh", None),
        P("mesh", None),
    )
    return jax.shard_map(
        shards,
        mesh=mesh,
        in_specs=placed,
        out_specs=(P("mesh", "band"), P("mesh", "band")),
        check_vma=False,
    )
```

```python
import jax
import jax.numpy as jnp
from jax import lax
from jax.experimental import pallas as pl
from jax.experimental.pallas import tpu as pltpu
from jax.sharding import PartitionSpec as P


APC = 8
FLIPS = (0, 1, 3, 2)
F32 = jnp.float32
BF16 = jnp.bfloat16
LANES = 128

filter_scale = 0.6
filter_shift = 1.0

VMEM = pl.BlockSpec(memory_space=pltpu.VMEM)
SMEM = pl.BlockSpec(memory_space=pltpu.SMEM)


def from_behind(block, axis, distance):
    devices = range(lax.axis_size(axis))
    route = [(i - distance, i) for i in devices if i - distance in devices]
    return lax.ppermute(block, axis, route)


def dot(a, b):
    return jnp.dot(a, b, preferred_element_type=F32)


def column(row):
    n = row.shape[1]
    parts = [
        jnp.transpose(jnp.broadcast_to(row[:, i : i + LANES], (LANES, LANES)))
        for i in range(0, n, LANES)
    ]
    return jnp.concatenate(parts, axis=0)


def widen(col, width):
    return jnp.concatenate([col] * (width // LANES), axis=1)


def hot_rows(row, width):
    col = column(row.astype(F32)).astype(jnp.int32)
    lane = lax.broadcasted_iota(jnp.int32, col.shape, 1)
    parts = [(col == lane + i).astype(F32).astype(BF16) for i in range(0, width, LANES)]
    return jnp.concatenate(parts, axis=1)


def hot_columns(row, height):
    n = row.shape[1]
    line = lax.broadcasted_iota(jnp.int32, (height, n), 0)
    return (line == row).astype(F32).astype(BF16)


def split_rows(row):
    high = row.astype(BF16).astype(F32)
    middle = (row - high).astype(BF16).astype(F32)
    low = row - high - middle
    line = lax.broadcasted_iota(jnp.int32, (16, row.shape[1]), 0)
    parts = jnp.where(line == 0, high, jnp.where(line == 1, middle, jnp.where(line == 2, low, 0.0)))
    return parts.astype(BF16)


def is_left():
    return lax.rem(lax.axis_index("mesh"), 2) == 0


def start_kernel(state, mass, send, coupling, scaled, outgoing, flags, strengths):
    here = lax.axis_index("mesh")
    inside = jnp.logical_and(here > 0, here < lax.axis_size("mesh") - 1)
    flags[0:8, :] = jnp.full((8, flags.shape[1]), jnp.where(is_left(), 1.0, 0.0), F32)
    flags[8:16, :] = jnp.full((8, flags.shape[1]), jnp.where(inside, 1.0, 0.0), F32)
    atoms, per_atom = coupling.shape
    width = atoms * per_atom
    spread = jnp.concatenate(
        [jnp.broadcast_to(coupling[a : a + 1, :], (per_atom, per_atom)) for a in range(atoms)], axis=0
    )
    line = lax.broadcasted_iota(jnp.int32, spread.shape, 0)
    lane = lax.broadcasted_iota(jnp.int32, spread.shape, 1)
    tall = jnp.sum(jnp.where(line % per_atom == lane, spread, 0.0), axis=1, keepdims=True)
    square = (width, width)
    diagonal = lax.broadcasted_iota(jnp.int32, square, 0) == lax.broadcasted_iota(jnp.int32, square, 1)
    row = jnp.sum(jnp.where(diagonal, jnp.broadcast_to(tall, square), 0.0), axis=0, keepdims=True)
    strengths[...] = jnp.concatenate([split_rows(row)] * (strengths.shape[1] // width), axis=1)
    m = widen(column(mass[...]), state.shape[1])
    scaled[...] = (m * state[...].astype(F32)).astype(BF16)
    face = send.shape[1]
    outgoing[0:face, :] = dot(hot_rows(send[...], state.shape[0]), scaled[...]).astype(BF16)
    outgoing[face : face + 16, :] = dot(
        split_rows(mass[...]), hot_columns(send[...], state.shape[0])
    ).astype(BF16)


def hot_kernel(nodes, pick, place):
    cells, per_cell = nodes.shape
    extended = place.shape[0]
    for c in range(cells):
        row = nodes[c : c + 1, :]
        pick[c * per_cell : (c + 1) * per_cell, :] = hot_rows(row, extended)
        place[:, c * per_cell : (c + 1) * per_cell] = hot_columns(row, extended)


def operator_kernel(potential, stiffness, shape_values, live, scale, operator):
    values = shape_values[...].astype(F32)
    turned = jnp.transpose(shape_values[...])
    for c in range(potential.shape[0]):
        points = column(potential[c : c + 1, :])
        weighted = (widen(points, values.shape[1]) * values).astype(BF16)
        alive = jnp.where(c < live[0], 1.0, 0.0)
        local = 0.5 * scale[c] * stiffness[...].astype(F32) + dot(turned, weighted)
        operator[c] = (alive * local).astype(BF16)


def store_sums(table, field, sums, first):
    sums[...] = dot(table[...], field[...]).astype(BF16)
    block = sums.shape[0] // 5
    first[0:block, :] = jnp.where(is_left(), sums[4 * block :, :], sums[0:block, :])


def table_kernel(
    projectors, pick, owner, slot, live, ghost, scaled, strengths,
    table, sums, first, wide, field, nodes,
):
    here, x = lax.axis_index("mesh"), lax.axis_index("band") // 2
    cells, per_atom = owner.shape[0], table.shape[0] // (5 * APC)
    per_cell = pick.shape[0] // cells
    share = projectors.shape[3]
    face = scaled.shape[0] // 4
    wide[...] = jnp.zeros_like(wide)
    field[0:face, :] = ghost[0:face, :]
    field[face:, :] = scaled[...]
    for c in range(cells):
        for i, flip in enumerate(FLIPS):
            for core in range(2):
                band = (x ^ flip) * 2 + core
                rows = pl.ds(pl.multiple_of(band * share, share), share)
                nodes[rows, :] = projectors[core, i, c].astype(F32)
        block = jnp.transpose(nodes[...]).astype(BF16)
        at_nodes = dot(block, pick[c * per_cell : (c + 1) * per_cell, :])
        at_nodes = at_nodes * jnp.where(c < live[0], 1.0, 0.0)
        for j in range(APC):
            target = (owner[c, j] - here + 2) * APC + slot[c, j]
            rows = pl.ds(pl.multiple_of(target * per_atom, per_atom), per_atom)
            wide[rows, :] = wide[rows, :] + at_nodes[per_atom * j : per_atom * (j + 1), :]
    table[...] = wide[...].astype(BF16)
    store_sums(table, field, sums, first)
    first[first.shape[0] - 16 :, :] = strengths[...]


def turn_kernel(table, turned):
    turned[...] = jnp.transpose(table[...])


def gather_kernel(pick, operator, ghost, scaled, terms, field):
    face = scaled.shape[0] // 4
    cells, per_cell = operator.shape[0], operator.shape[1]
    field[0:face, :] = ghost[0:face, :]
    field[face:, :] = scaled[...]
    for c in range(cells):
        rows = slice(c * per_cell, (c + 1) * per_cell)
        cell = dot(pick[rows, :], field[...]).astype(BF16)
        terms[rows, :] = dot(operator[c], cell).astype(BF16)


def scatter_kernel(place, terms, out):
    out[...] = dot(place[...], terms[...])


def couple_kernel(both, strengths, came, pair):
    block = pair.shape[1]

    def tall(rows):
        split = rows[...].astype(F32)
        return column(split[0:1, 0:block] + split[1:2, 0:block] + split[2:3, 0:block])

    mine, other = tall(strengths), tall(came.at[block : block + 16, :])
    left = is_left()
    for i in range(2):
        at = slice(i * block, (i + 1) * block)
        total = both[0, at, :].astype(F32) + both[1, at, :].astype(F32)
        factor = jnp.where(left, mine, other) if i == 0 else jnp.where(left, other, mine)
        pair[i] = (widen(factor, total.shape[1]) * total).astype(BF16)


def apply_out(turned, values, local):
    return local[...] + dot(turned[...], values[...])


def middle_kernel(
    turned, values, local, state, prev, mass, send, returned, own, edge
):
    face = send.shape[1]
    total = apply_out(turned, values, local)
    returned[...] = total[0:face, :].astype(BF16)
    own[...] = total[face:, :]
    m = widen(column(mass[...]), state.shape[1])
    current = state[...].astype(F32)
    partial = filter_scale * (m * own[...] - filter_shift * current) - prev[...].astype(F32)
    edge[...] = dot(hot_rows(send[...], state.shape[0]), (m * partial).astype(BF16)).astype(BF16)


def next_kernel(
    own, received, edge, returned, ghost, state, prev, mass, send, table,
    first, scaled, ghost_next, sums, sent, field,
):
    face = send.shape[1]
    m = widen(column(mass[...]), state.shape[1])
    owned = own[...] + dot(hot_columns(send[...], state.shape[0]), received[...])
    current = state[...].astype(F32)
    one = filter_scale * (m * owned - filter_shift * current) - prev[...].astype(F32)
    first[...] = one.astype(BF16)
    scaled[...] = (m * first[...].astype(F32)).astype(BF16)
    split = ghost[face : face + 16, :].astype(F32)
    g = widen(column(split[0:1, :] + split[1:2, :] + split[2:3, :]), state.shape[1])
    ghost_next[...] = (
        edge[...].astype(F32) + (filter_scale * g * g) * returned[...].astype(F32)
    ).astype(BF16)
    field[0:face, :] = ghost_next[...]
    field[face:, :] = scaled[...]
    store_sums(table, field, sums, sent)


def end_kernel(turned, values, local, returned, own):
    face = returned.shape[0]
    total = apply_out(turned, values, local)
    returned[...] = total[0:face, :].astype(BF16)
    own[...] = total[face:, :]


def last_kernel(own, received, state, first, mass, send, second):
    m = widen(column(mass[...]), state.shape[1])
    owned = own[...] + dot(hot_columns(send[...], state.shape[0]), received[...])
    two = filter_scale * (m * owned - filter_shift * first[...].astype(F32))
    second[...] = (two - state[...].astype(F32)).astype(BF16)


def call(kernel, outs, args, specs=None, scratch=(), mib=8):
    return pl.pallas_call(
        kernel,
        out_shape=[
            kept[0](*kept[1:]) if kept else jax.ShapeDtypeStruct(shape, kind)
            for shape, kind, *kept in outs
        ],
        in_specs=specs or [VMEM] * len(args),
        out_specs=[VMEM] * len(outs),
        scratch_shapes=list(scratch),
        compiler_params=pltpu.CompilerParams(vmem_limit_bytes=mib << 20),
    )(*args)


def kept(shape, kind):
    return (shape, kind, pltpu.VMEM, shape, kind)


def hold(block):
    return pltpu.with_memory_space_constraint(block, pltpu.VMEM)


def inner_pairs(block):
    n = lax.axis_size("mesh")
    groups = [[i, i + 1] for i in range(0, n, 2)]
    return lax.all_gather(block, "mesh", axis=0, axis_index_groups=groups)


def outer_pairs(block):
    n, m = lax.axis_size("mesh"), lax.axis_size("band")
    groups = [[i * m + k, (i + 1) * m + k] for i in range(1, n - 1, 2) for k in range(m)]
    groups += [[i * m + k, i * m + k + 1] for i in (0, n - 1) for k in range(0, m, 2)]
    return lax.all_gather(block, ("mesh", "band"), axis=0, axis_index_groups=groups)


def swap(block, axis, mask):
    return lax.ppermute(block, axis, [(i, i ^ mask) for i in range(lax.axis_size(axis))])


def shards(
    state,
    prev_state,
    mass,
    cell_nodes,
    cell_live,
    cell_scale,
    potential,
    stiffness,
    shape_values,
    cell_proj,
    cell_owner,
    cell_slot,
    coupling,
    send_rows,
):
    own_rows, orbitals = state.shape
    cells, per_cell = cell_nodes.shape
    atoms, per_atom = coupling.shape
    face = send_rows.shape[1]
    extended = own_rows + face
    block = atoms * per_atom
    window = 5 * block
    mass_row = mass.reshape(1, own_rows)
    scaled, outgoing, flags, strengths = call(
        start_kernel,
        [
            ((own_rows, orbitals), BF16),
            ((face + 16, orbitals), BF16),
            ((16, orbitals), F32),
            ((16, orbitals), BF16),
        ],
        (state, mass_row, send_rows, coupling),
    )
    left = flags[0:1] > 0.5
    inside = flags[8:9] > 0.5
    ghost = from_behind(outgoing, "mesh", 1)

    other = swap(cell_proj, "band", 2)
    pick, place = call(
        hot_kernel,
        [kept((cells * per_cell, extended), BF16), kept((extended, cells * per_cell), BF16)],
        (cell_nodes,),
    )
    pick, place = hold(pick), hold(place)
    near = jnp.stack([cell_proj, other])
    far = swap(near, "band", 6)
    (operator,) = call(
        operator_kernel,
        [kept((cells, per_cell, per_cell), BF16)],
        (potential, stiffness, shape_values, cell_live, cell_scale),
        specs=[VMEM, VMEM, VMEM, SMEM, SMEM],
    )
    operator = hold(operator)
    projectors = lax.all_gather(
        jnp.concatenate([near, far], axis=0),
        "band",
        axis=0,
        axis_index_groups=[[0, 1], [2, 3], [4, 5], [6, 7]],
    )

    part = ((block, orbitals), BF16)
    block_of = ((block, orbitals), BF16)
    window_of = ((window, orbitals), BF16)
    table, sums, sent = call(
        table_kernel,
        [kept((window, extended), BF16), window_of, ((block + 16, orbitals), BF16)],
        (projectors, pick, cell_owner, cell_slot, cell_live, ghost, scaled, strengths),
        specs=[VMEM, VMEM, SMEM, SMEM, SMEM, VMEM, VMEM, VMEM],
        scratch=[
            pltpu.VMEM((window, extended), F32),
            pltpu.VMEM((extended, orbitals), BF16),
            pltpu.VMEM((per_cell, block), F32),
        ],
    )
    table = hold(table)
    (turned,) = call(turn_kernel, [kept((extended, window), BF16)], (table,))
    turned = hold(turned)

    def atom_values(sums, sent, terms, came):
        at = [sums[i * block : (i + 1) * block].astype(F32) for i in range(5)]
        got, terms = lax.optimization_barrier((swap(sent, "mesh", 1), terms))
        came = got if came is None else came
        added = got[:block].astype(F32)
        outward = jnp.concatenate(
            [
                jnp.where(left, at[0], at[3] + added),
                jnp.where(left, at[1] + added, at[4]),
            ]
        ).astype(BF16)
        both = outer_pairs(outward)
        inward = jnp.where(left, both[0], both[1]).astype(F32)
        mine = jnp.concatenate(
            [jnp.where(left, at[2], at[1]), jnp.where(left, at[3], at[2])]
        ) + jnp.where(inside, inward, 0.0)
        both = inner_pairs(mine.astype(BF16))
        (pair,) = call(
            couple_kernel, [((2, block, orbitals), BF16)], (both, strengths, came)
        )
        both = outer_pairs(pair.reshape(2 * block, orbitals))
        beside = jnp.where(left, both[0], both[1])
        both = inner_pairs(jnp.where(left, beside[block:], beside[:block]))
        beyond = jnp.where(left, both[1], both[0])
        values = jnp.concatenate(
            [
                jnp.where(left, beside[:block], beyond),
                jnp.where(left, beside[block:], pair[0]),
                jnp.where(left, pair[0], pair[1]),
                jnp.where(left, pair[1], beside[:block]),
                jnp.where(left, beyond, beside[block:]),
            ]
        )
        (local,) = call(scatter_kernel, [((extended, orbitals), F32)], (place, terms))
        return values, local, came

    def cell_terms(ghost, scaled):
        (terms,) = call(
            gather_kernel,
            [((cells * per_cell, orbitals), BF16)],
            (pick, operator, ghost, scaled),
            scratch=[pltpu.VMEM((extended, orbitals), BF16)],
        )
        return terms

    nodal = ((own_rows, orbitals), BF16)
    shared = ((face, orbitals), BF16)
    own_wide = ((own_rows, orbitals), F32)

    values, local, came = atom_values(sums, sent, cell_terms(ghost, scaled), None)
    returned, own, edge = call(
        middle_kernel,
        [shared, own_wide, shared],
        (turned, values, local, state, prev_state, mass_row, send_rows),
    )
    received = from_behind(returned, "mesh", -1)
    edge_in = from_behind(edge, "mesh", 1)
    first, scaled_one, ghost_one, sums_one, sent_one = call(
        next_kernel,
        [nodal, nodal, shared, window_of, block_of],
        (own, received, edge_in, returned, ghost, state, prev_state, mass_row, send_rows, table),
        scratch=[pltpu.VMEM((extended, orbitals), BF16)],
    )
    terms_one = cell_terms(ghost_one, scaled_one)
    values_one, local_one, _ = atom_values(sums_one, sent_one, terms_one, came)
    returned_one, own_one = call(
        end_kernel, [shared, own_wide], (turned, values_one, local_one)
    )
    received_one = from_behind(returned_one, "mesh", -1)
    (second,) = call(
        last_kernel, [nodal], (own_one, received_one, state, first, mass_row, send_rows)
    )
    return (first, second)


def solution(mesh):
    placed = (
        P("mesh", "band"),
        P("mesh", "band"),
        P("mesh"),
        P("mesh", None),
        P("mesh"),
        P("mesh"),
        P("mesh", None),
        P(),
        P(),
        P("mesh", "band", None),
        P("mesh", None),
        P("mesh", None),
        P("mesh", None),
        P("mesh", None),
    )
    return jax.shard_map(
        shards,
        mesh=mesh,
        in_specs=placed,
        out_specs=(P("mesh", "band"), P("mesh", "band")),
        check_vma=False,
    )
```

```python
import jax
import jax.numpy as jnp
from jax import lax
from jax.experimental import pallas as pl
from jax.experimental.pallas import tpu as pltpu
from jax.sharding import PartitionSpec as P


APC = 8
FLIPS = (0, 1, 3, 2)
F32 = jnp.float32
BF16 = jnp.bfloat16
LANES = 128

filter_scale = 0.6
filter_shift = 1.0

VMEM = pl.BlockSpec(memory_space=pltpu.VMEM)
SMEM = pl.BlockSpec(memory_space=pltpu.SMEM)


def from_behind(block, axis, distance):
    devices = range(lax.axis_size(axis))
    route = [(i - distance, i) for i in devices if i - distance in devices]
    return lax.ppermute(block, axis, route)


def dot(a, b):
    return jnp.dot(a, b, preferred_element_type=F32)


def column(row):
    n = row.shape[1]
    parts = [
        jnp.transpose(jnp.broadcast_to(row[:, i : i + LANES], (LANES, LANES)))
        for i in range(0, n, LANES)
    ]
    return jnp.concatenate(parts, axis=0)


def widen(col, width):
    return jnp.concatenate([col] * (width // LANES), axis=1)


def hot_rows(row, width):
    col = column(row.astype(F32)).astype(jnp.int32)
    lane = lax.broadcasted_iota(jnp.int32, col.shape, 1)
    parts = [(col == lane + i).astype(F32).astype(BF16) for i in range(0, width, LANES)]
    return jnp.concatenate(parts, axis=1)


def hot_columns(row, height):
    n = row.shape[1]
    line = lax.broadcasted_iota(jnp.int32, (height, n), 0)
    return (line == row).astype(F32).astype(BF16)


def split_rows(row):
    high = row.astype(BF16).astype(F32)
    middle = (row - high).astype(BF16).astype(F32)
    low = row - high - middle
    line = lax.broadcasted_iota(jnp.int32, (16, row.shape[1]), 0)
    parts = jnp.where(line == 0, high, jnp.where(line == 1, middle, jnp.where(line == 2, low, 0.0)))
    return parts.astype(BF16)


def is_left():
    return lax.rem(lax.axis_index("mesh"), 2) == 0


def start_kernel(state, mass, send, coupling, scaled, outgoing, strengths):
    atoms, per_atom = coupling.shape
    width = atoms * per_atom
    spread = jnp.concatenate(
        [jnp.broadcast_to(coupling[a : a + 1, :], (per_atom, per_atom)) for a in range(atoms)], axis=0
    )
    line = lax.broadcasted_iota(jnp.int32, spread.shape, 0)
    lane = lax.broadcasted_iota(jnp.int32, spread.shape, 1)
    tall = jnp.sum(jnp.where(line % per_atom == lane, spread, 0.0), axis=1, keepdims=True)
    square = (width, width)
    diagonal = lax.broadcasted_iota(jnp.int32, square, 0) == lax.broadcasted_iota(jnp.int32, square, 1)
    row = jnp.sum(jnp.where(diagonal, jnp.broadcast_to(tall, square), 0.0), axis=0, keepdims=True)
    strengths[...] = jnp.concatenate([split_rows(row)] * (strengths.shape[1] // width), axis=1)
    m = widen(column(mass[...]), state.shape[1])
    scaled[...] = (m * state[...].astype(F32)).astype(BF16)
    face = send.shape[1]
    outgoing[0:face, :] = dot(hot_rows(send[...], state.shape[0]), scaled[...]).astype(BF16)
    outgoing[face : face + 16, :] = dot(
        split_rows(mass[...]), hot_columns(send[...], state.shape[0])
    ).astype(BF16)


def hot_kernel(nodes, pick, place):
    cells, per_cell = nodes.shape
    extended = place.shape[0]
    for c in range(cells):
        row = nodes[c : c + 1, :]
        pick[c * per_cell : (c + 1) * per_cell, :] = hot_rows(row, extended)
        place[:, c * per_cell : (c + 1) * per_cell] = hot_columns(row, extended)


def operator_kernel(potential, stiffness, shape_values, live, scale, operator):
    values = shape_values[...].astype(F32)
    turned = jnp.transpose(shape_values[...])
    for c in range(potential.shape[0]):
        points = column(potential[c : c + 1, :])
        weighted = (widen(points, values.shape[1]) * values).astype(BF16)
        alive = jnp.where(c < live[0], 1.0, 0.0)
        local = 0.5 * scale[c] * stiffness[...].astype(F32) + dot(turned, weighted)
        operator[c] = (alive * local).astype(BF16)


def store_sums(table, field, sent, outward, base):
    sums = dot(table[...], field[...])
    n = sent.shape[0]
    left = is_left()
    sent[...] = jnp.where(left, sums[4 * n :, :], sums[0:n, :]).astype(BF16)
    outward[...] = jnp.where(left, sums[0 : 2 * n, :], sums[3 * n :, :]).astype(BF16)
    base[...] = jnp.where(left, sums[2 * n : 4 * n, :], sums[n : 3 * n, :])


def table_kernel(
    projectors, pick, owner, slot, live, ghost, scaled,
    table, sent, outward, base, wide, field, nodes,
):
    here, x = lax.axis_index("mesh"), lax.axis_index("band") // 2
    cells, per_atom = owner.shape[0], table.shape[0] // (5 * APC)
    per_cell = pick.shape[0] // cells
    share = projectors.shape[3]
    face = scaled.shape[0] // 4
    wide[...] = jnp.zeros_like(wide)
    field[0:face, :] = ghost[0:face, :]
    field[face:, :] = scaled[...]
    for c in range(cells):
        for i, flip in enumerate(FLIPS):
            for core in range(2):
                band = (x ^ flip) * 2 + core
                rows = pl.ds(pl.multiple_of(band * share, share), share)
                nodes[rows, :] = projectors[core, i, c].astype(F32)
        block = jnp.transpose(nodes[...]).astype(BF16)
        at_nodes = dot(block, pick[c * per_cell : (c + 1) * per_cell, :])
        at_nodes = at_nodes * jnp.where(c < live[0], 1.0, 0.0)
        for j in range(APC):
            target = (owner[c, j] - here + 2) * APC + slot[c, j]
            rows = pl.ds(pl.multiple_of(target * per_atom, per_atom), per_atom)
            wide[rows, :] = wide[rows, :] + at_nodes[per_atom * j : per_atom * (j + 1), :]
    table[...] = wide[...].astype(BF16)
    store_sums(table, field, sent, outward, base)


def turn_kernel(table, turned):
    turned[...] = jnp.transpose(table[...])


def gather_kernel(pick, operator, ghost, scaled, terms, field):
    face = scaled.shape[0] // 4
    cells, per_cell = operator.shape[0], operator.shape[1]
    field[0:face, :] = ghost[0:face, :]
    field[face:, :] = scaled[...]
    for c in range(cells):
        rows = slice(c * per_cell, (c + 1) * per_cell)
        cell = dot(pick[rows, :], field[...]).astype(BF16)
        terms[rows, :] = dot(operator[c], cell).astype(BF16)


def scatter_kernel(place, terms, out):
    out[...] = dot(place[...], terms[...])


def join_kernel(base, both, far, strengths, mine, message):
    n = far.shape[0]
    left = is_left()
    here = lax.axis_index("mesh")
    inside = jnp.logical_and(here > 0, here < lax.axis_size("mesh") - 1)
    inward = jnp.where(left, both[0], both[1]).astype(F32)
    total = base[...] + jnp.where(inside, inward, 0.0)
    added = far[...].astype(F32)
    mine[0:n, :] = total[0:n, :] + jnp.where(left, added, 0.0)
    mine[n:, :] = total[n:, :] + jnp.where(left, 0.0, added)
    message[0 : 2 * n, :] = mine[...].astype(BF16)
    message[2 * n :, :] = strengths[...]


def couple_kernel(mine, message, strengths, pair, sent):
    n = sent.shape[0]

    def tall(rows):
        split = rows[...].astype(F32)
        return column(split[0:1, 0:n] + split[1:2, 0:n] + split[2:3, 0:n])

    own, other = tall(strengths), tall(message.at[2 * n : 2 * n + 16, :])
    left = is_left()
    for i in range(2):
        at = slice(i * n, (i + 1) * n)
        total = mine[at, :] + message[at, :].astype(F32)
        factor = jnp.where(left, own, other) if i == 0 else jnp.where(left, other, own)
        pair[at, :] = (widen(factor, total.shape[1]) * total).astype(BF16)
    sent[...] = jnp.where(left, pair[0:n, :], pair[n:, :])


def window_values(pair, both, far):
    left = is_left()
    n = far.shape[0]
    beside = jnp.where(left, both[0], both[1])
    return jnp.concatenate(
        [
            jnp.where(left, beside[0:n], far[...]),
            jnp.where(left, beside[n:], pair[0:n, :]),
            jnp.where(left, pair[0:n, :], pair[n:, :]),
            jnp.where(left, pair[n:, :], beside[0:n]),
            jnp.where(left, far[...], beside[n:]),
        ]
    )


def apply_out(turned, pair, both, far, local):
    return local[...] + dot(turned[...], window_values(pair, both, far))


def middle_kernel(
    turned, pair, both, far, local, state, prev, mass, send, returned, own, edge, message
):
    face = send.shape[1]
    total = apply_out(turned, pair, both, far, local)
    returned[...] = total[0:face, :].astype(BF16)
    own[...] = total[face:, :]
    m = widen(column(mass[...]), state.shape[1])
    current = state[...].astype(F32)
    partial = filter_scale * (m * own[...] - filter_shift * current) - prev[...].astype(F32)
    edge[...] = dot(hot_rows(send[...], state.shape[0]), (m * partial).astype(BF16)).astype(BF16)
    left = is_left()
    message[0] = jnp.where(left, edge[...], returned[...])
    message[1] = jnp.where(left, returned[...], edge[...])


def next_kernel(
    own, inner, outer, returned, ghost, state, prev, mass, send, table,
    first, scaled, ghost_next, sent, outward, base, field,
):
    face = send.shape[1]
    m = widen(column(mass[...]), state.shape[1])
    left = is_left()
    within = jnp.where(left, inner[1], inner[0])
    received = jnp.where(left, within, outer[...])
    edge = jnp.where(left, outer[...], within)
    owned = own[...] + dot(hot_columns(send[...], state.shape[0]), received)
    current = state[...].astype(F32)
    one = filter_scale * (m * owned - filter_shift * current) - prev[...].astype(F32)
    first[...] = one.astype(BF16)
    scaled[...] = (m * first[...].astype(F32)).astype(BF16)
    split = ghost[face : face + 16, :].astype(F32)
    g = widen(column(split[0:1, :] + split[1:2, :] + split[2:3, :]), state.shape[1])
    ghost_next[...] = (
        edge.astype(F32) + (filter_scale * g * g) * returned[...].astype(F32)
    ).astype(BF16)
    field[0:face, :] = ghost_next[...]
    field[face:, :] = scaled[...]
    store_sums(table, field, sent, outward, base)


def end_kernel(turned, pair, both, far, local, returned, own):
    face = returned.shape[0]
    total = apply_out(turned, pair, both, far, local)
    returned[...] = total[0:face, :].astype(BF16)
    own[...] = total[face:, :]


def last_kernel(own, received, state, first, mass, send, second):
    m = widen(column(mass[...]), state.shape[1])
    owned = own[...] + dot(hot_columns(send[...], state.shape[0]), received[...])
    two = filter_scale * (m * owned - filter_shift * first[...].astype(F32))
    second[...] = (two - state[...].astype(F32)).astype(BF16)


def call(kernel, outs, args, specs=None, scratch=(), mib=8):
    return pl.pallas_call(
        kernel,
        out_shape=[
            kept[0](*kept[1:]) if kept else jax.ShapeDtypeStruct(shape, kind)
            for shape, kind, *kept in outs
        ],
        in_specs=specs or [VMEM] * len(args),
        out_specs=[VMEM] * len(outs),
        scratch_shapes=list(scratch),
        compiler_params=pltpu.CompilerParams(vmem_limit_bytes=mib << 20),
    )(*args)


def kept(shape, kind):
    return (shape, kind, pltpu.VMEM, shape, kind)


def hold(block):
    return pltpu.with_memory_space_constraint(block, pltpu.VMEM)


def leave(block):
    return pltpu.with_memory_space_constraint(block, pltpu.HBM)


def inner_pairs(block):
    n = lax.axis_size("mesh")
    groups = [[i, i + 1] for i in range(0, n, 2)]
    return lax.all_gather(block, "mesh", axis=0, axis_index_groups=groups)


def outer_pairs(block):
    n, m = lax.axis_size("mesh"), lax.axis_size("band")
    groups = [[i * m + k, (i + 1) * m + k] for i in range(1, n - 1, 2) for k in range(m)]
    groups += [[i * m + k, i * m + k + 1] for i in (0, n - 1) for k in range(0, m, 2)]
    return lax.all_gather(block, ("mesh", "band"), axis=0, axis_index_groups=groups)


def outer_swap(block):
    n = lax.axis_size("mesh")
    route = [(i, i + 1 if i % 2 else i - 1) for i in range(1, n - 1)]
    return lax.ppermute(block, "mesh", route)


def two_away(block, way):
    n = lax.axis_size("mesh")
    route = [(i, i + (2 * way if i % 2 == 0 else -2 * way)) for i in range(n)]
    return lax.ppermute(block, "mesh", [(i, j) for i, j in route if 0 <= j < n])


def swap(block, axis, mask):
    return lax.ppermute(block, axis, [(i, i ^ mask) for i in range(lax.axis_size(axis))])


def shards(
    state,
    prev_state,
    mass,
    cell_nodes,
    cell_live,
    cell_scale,
    potential,
    stiffness,
    shape_values,
    cell_proj,
    cell_owner,
    cell_slot,
    coupling,
    send_rows,
):
    own_rows, orbitals = state.shape
    cells, per_cell = cell_nodes.shape
    atoms, per_atom = coupling.shape
    face = send_rows.shape[1]
    extended = own_rows + face
    block = atoms * per_atom
    window = 5 * block
    mass_row = mass.reshape(1, own_rows)
    other = swap(cell_proj, "band", 2)
    start = call
    scaled, outgoing, strengths = start(
        start_kernel,
        [
            ((own_rows, orbitals), BF16),
            ((face + 16, orbitals), BF16),
            ((16, orbitals), BF16),
        ],
        [leave(block) for block in (state, mass_row, send_rows, coupling)],
    )
    ghost = from_behind(outgoing, "mesh", 1)

    pick, place = call(
        hot_kernel,
        [kept((cells * per_cell, extended), BF16), kept((extended, cells * per_cell), BF16)],
        (leave(cell_nodes),),
    )
    pick, place = hold(pick), hold(place)
    near = jnp.stack([cell_proj, other])
    far = swap(near, "band", 6)
    (operator,) = call(
        operator_kernel,
        [kept((cells, per_cell, per_cell), BF16)],
        (leave(potential), leave(stiffness), leave(shape_values), cell_live, cell_scale),
        specs=[VMEM, VMEM, VMEM, SMEM, SMEM],
    )
    operator = hold(operator)
    projectors = lax.all_gather(
        jnp.concatenate([near, far], axis=0),
        "band",
        axis=0,
        axis_index_groups=[[0, 1], [2, 3], [4, 5], [6, 7]],
    )

    sums_of = [((block, orbitals), BF16), ((2 * block, orbitals), BF16), ((2 * block, orbitals), F32)]
    table, *sums = call(
        table_kernel,
        [kept((window, extended), BF16)] + sums_of,
        (projectors, pick, cell_owner, cell_slot, cell_live, ghost, scaled),
        specs=[VMEM, VMEM, SMEM, SMEM, SMEM, VMEM, VMEM],
        scratch=[
            pltpu.VMEM((window, extended), F32),
            pltpu.VMEM((extended, orbitals), BF16),
            pltpu.VMEM((per_cell, block), F32),
        ],
    )
    table = hold(table)
    (turned,) = call(turn_kernel, [kept((extended, window), BF16)], (table,))
    turned = hold(turned)

    def atom_values(sums, terms):
        sent, outward, base = sums
        far = two_away(sent, 1)
        both = outer_pairs(outward)
        mine, message = call(
            join_kernel,
            [((2 * block, orbitals), F32), ((2 * block + 16, orbitals), BF16)],
            (base, both, far, strengths),
        )
        message, terms = lax.optimization_barrier((swap(message, "mesh", 1), terms))
        pair, sent = call(
            couple_kernel,
            [((2 * block, orbitals), BF16), ((block, orbitals), BF16)],
            (mine, message, strengths),
        )
        far = two_away(sent, -1)
        both = outer_pairs(pair)
        (local,) = call(scatter_kernel, [((extended, orbitals), F32)], (place, terms))
        return (pair, both, far), local

    def cell_terms(ghost, scaled):
        (terms,) = call(
            gather_kernel,
            [((cells * per_cell, orbitals), BF16)],
            (pick, operator, ghost, scaled),
            scratch=[pltpu.VMEM((extended, orbitals), BF16)],
        )
        return terms

    nodal = ((own_rows, orbitals), BF16)
    shared = ((face, orbitals), BF16)
    own_wide = ((own_rows, orbitals), F32)

    values, local = atom_values(sums, cell_terms(ghost, scaled))
    returned, own, _, message = call(
        middle_kernel,
        [shared, own_wide, shared, ((2, face, orbitals), BF16)],
        (turned, *values, local, state, prev_state, mass_row, send_rows),
    )
    outer = outer_swap(message[1])
    inner = inner_pairs(message[0])
    first, scaled_one, ghost_one, *sums_one = call(
        next_kernel,
        [nodal, nodal, shared] + sums_of,
        (own, inner, outer, returned, ghost, state, prev_state, mass_row, send_rows, table),
        scratch=[pltpu.VMEM((extended, orbitals), BF16)],
    )
    terms_one = cell_terms(ghost_one, scaled_one)
    values_one, local_one = atom_values(sums_one, terms_one)
    returned_one, own_one = call(
        end_kernel, [shared, own_wide], (turned, *values_one, local_one)
    )
    received_one = from_behind(returned_one, "mesh", -1)
    (second,) = call(
        last_kernel, [nodal], (own_one, received_one, state, first, mass_row, send_rows)
    )
    return (first, second)


def solution(mesh):
    placed = (
        P("mesh", "band"),
        P("mesh", "band"),
        P("mesh"),
        P("mesh", None),
        P("mesh"),
        P("mesh"),
        P("mesh", None),
        P(),
        P(),
        P("mesh", "band", None),
        P("mesh", None),
        P("mesh", None),
        P("mesh", None),
        P("mesh", None),
    )

    return jax.shard_map(
        shards,
        mesh=mesh,
        in_specs=placed,
        out_specs=(P("mesh", "band"), P("mesh", "band")),
        check_vma=False,
    )
```

```python
import jax
import jax.numpy as jnp
from jax import lax
from jax.experimental import pallas as pl
from jax.experimental.pallas import tpu as pltpu
from jax.sharding import PartitionSpec as P


APC = 8
FLIPS = (0, 1, 3, 2)
F32 = jnp.float32
BF16 = jnp.bfloat16
LANES = 128

filter_scale = 0.6
filter_shift = 1.0

VMEM = pl.BlockSpec(memory_space=pltpu.VMEM)
SMEM = pl.BlockSpec(memory_space=pltpu.SMEM)


def from_behind(block, axis, distance):
    devices = range(lax.axis_size(axis))
    route = [(i - distance, i) for i in devices if i - distance in devices]
    return lax.ppermute(block, axis, route)


def dot(a, b):
    return jnp.dot(a, b, preferred_element_type=F32)


def column(row):
    n = row.shape[1]
    parts = [
        jnp.transpose(jnp.broadcast_to(row[:, i : i + LANES], (LANES, LANES)))
        for i in range(0, n, LANES)
    ]
    return jnp.concatenate(parts, axis=0)


def widen(col, width):
    return jnp.concatenate([col] * (width // LANES), axis=1)


def hot_rows(row, width):
    col = column(row.astype(F32)).astype(jnp.int32)
    lane = lax.broadcasted_iota(jnp.int32, col.shape, 1)
    parts = [(col == lane + i).astype(F32).astype(BF16) for i in range(0, width, LANES)]
    return jnp.concatenate(parts, axis=1)


def hot_columns(row, height):
    n = row.shape[1]
    line = lax.broadcasted_iota(jnp.int32, (height, n), 0)
    return (line == row).astype(F32).astype(BF16)


def split_rows(row):
    high = row.astype(BF16).astype(F32)
    middle = (row - high).astype(BF16).astype(F32)
    low = row - high - middle
    line = lax.broadcasted_iota(jnp.int32, (16, row.shape[1]), 0)
    parts = jnp.where(line == 0, high, jnp.where(line == 1, middle, jnp.where(line == 2, low, 0.0)))
    return parts.astype(BF16)


def is_left():
    return lax.rem(lax.axis_index("mesh"), 2) == 0


def start_kernel(state, mass, send, coupling, scaled, outgoing, strengths):
    atoms, per_atom = coupling.shape
    width = atoms * per_atom
    spread = jnp.concatenate(
        [jnp.broadcast_to(coupling[a : a + 1, :], (per_atom, per_atom)) for a in range(atoms)], axis=0
    )
    line = lax.broadcasted_iota(jnp.int32, spread.shape, 0)
    lane = lax.broadcasted_iota(jnp.int32, spread.shape, 1)
    tall = jnp.sum(jnp.where(line % per_atom == lane, spread, 0.0), axis=1, keepdims=True)
    square = (width, width)
    diagonal = lax.broadcasted_iota(jnp.int32, square, 0) == lax.broadcasted_iota(jnp.int32, square, 1)
    row = jnp.sum(jnp.where(diagonal, jnp.broadcast_to(tall, square), 0.0), axis=0, keepdims=True)
    strengths[...] = jnp.concatenate([split_rows(row)] * (strengths.shape[1] // width), axis=1)
    m = widen(column(mass[...]), state.shape[1])
    scaled[...] = (m * state[...].astype(F32)).astype(BF16)
    face = send.shape[1]
    outgoing[0:face, :] = dot(hot_rows(send[...], state.shape[0]), scaled[...]).astype(BF16)
    outgoing[face : face + 16, :] = dot(
        split_rows(mass[...]), hot_columns(send[...], state.shape[0])
    ).astype(BF16)


def pick_kernel(nodes, pick):
    cells, per_cell = nodes.shape
    for c in range(cells):
        row = nodes[c : c + 1, :]
        pick[c * per_cell : (c + 1) * per_cell, :] = hot_rows(row, pick.shape[1])


def place_kernel(nodes, place):
    cells, per_cell = nodes.shape
    for c in range(cells):
        row = nodes[c : c + 1, :]
        place[:, c * per_cell : (c + 1) * per_cell] = hot_columns(row, place.shape[0])


def operator_kernel(potential, stiffness, shape_values, live, scale, operator):
    values = shape_values[...].astype(F32)
    turned = jnp.transpose(shape_values[...])
    for c in range(potential.shape[0]):
        points = column(potential[c : c + 1, :])
        weighted = (widen(points, values.shape[1]) * values).astype(BF16)
        alive = jnp.where(c < live[0], 1.0, 0.0)
        local = 0.5 * scale[c] * stiffness[...].astype(F32) + dot(turned, weighted)
        operator[c] = (alive * local).astype(BF16)


def store_sums(table, field, sent, outward, base):
    sums = dot(table[...], field[...])
    n = sent.shape[0]
    left = is_left()
    sent[...] = jnp.where(left, sums[4 * n :, :], sums[0:n, :]).astype(BF16)
    outward[...] = jnp.where(left, sums[0 : 2 * n, :], sums[3 * n :, :]).astype(BF16)
    base[...] = jnp.where(left, sums[2 * n : 4 * n, :], sums[n : 3 * n, :])


def table_kernel(
    projectors, pick, owner, slot, live, ghost, scaled,
    table, sent, outward, base, wide, field, nodes,
):
    here, x = lax.axis_index("mesh"), lax.axis_index("band") // 2
    cells, per_atom = owner.shape[0], table.shape[0] // (5 * APC)
    per_cell = pick.shape[0] // cells
    share = projectors.shape[3]
    face = scaled.shape[0] // 4
    wide[...] = jnp.zeros_like(wide)
    field[0:face, :] = ghost[0:face, :]
    field[face:, :] = scaled[...]
    for c in range(cells):
        for i, flip in enumerate(FLIPS):
            for core in range(2):
                band = (x ^ flip) * 2 + core
                rows = pl.ds(pl.multiple_of(band * share, share), share)
                nodes[rows, :] = projectors[core, i, c].astype(F32)
        block = jnp.transpose(nodes[...]).astype(BF16)
        at_nodes = dot(block, pick[c * per_cell : (c + 1) * per_cell, :])
        at_nodes = at_nodes * jnp.where(c < live[0], 1.0, 0.0)
        for j in range(APC):
            target = (owner[c, j] - here + 2) * APC + slot[c, j]
            rows = pl.ds(pl.multiple_of(target * per_atom, per_atom), per_atom)
            wide[rows, :] = wide[rows, :] + at_nodes[per_atom * j : per_atom * (j + 1), :]
    table[...] = wide[...].astype(BF16)
    store_sums(table, field, sent, outward, base)


def turn_kernel(table, turned):
    turned[...] = jnp.transpose(table[...])


def gather_kernel(pick, operator, ghost, scaled, terms, field, held):
    face = scaled.shape[0] // 4
    cells, per_cell = operator.shape[0], operator.shape[1]
    field[0:face, :] = ghost[0:face, :]
    field[face:, :] = scaled[...]
    held[...] = dot(pick[...], field[...]).astype(BF16)
    for c in range(cells):
        rows = slice(c * per_cell, (c + 1) * per_cell)
        terms[rows, :] = dot(operator[c], held[rows, :]).astype(BF16)


def scatter_kernel(place, terms, out):
    out[...] = dot(place[...], terms[...])


def join_kernel(base, near, far, strengths, mine, message):
    n = far.shape[0]
    left = is_left()
    total = base[...] + near[...].astype(F32)
    added = far[...].astype(F32)
    mine[0:n, :] = total[0:n, :] + jnp.where(left, added, 0.0)
    mine[n:, :] = total[n:, :] + jnp.where(left, 0.0, added)
    message[0 : 2 * n, :] = mine[...].astype(BF16)
    message[2 * n :, :] = strengths[...]


def couple_kernel(mine, both, strengths, pair, sent):
    n = sent.shape[0]

    def tall(split):
        split = split.astype(F32)
        return column(split[0:1, 0:n] + split[1:2, 0:n] + split[2:3, 0:n])

    message = jnp.where(is_left(), both[1], both[0]).astype(F32)
    own, other = tall(strengths[...]), tall(message[2 * n :, :])
    left = is_left()
    for i in range(2):
        at = slice(i * n, (i + 1) * n)
        total = mine[at, :] + message[at, :]
        factor = jnp.where(left, own, other) if i == 0 else jnp.where(left, other, own)
        pair[at, :] = (widen(factor, total.shape[1]) * total).astype(BF16)
    sent[...] = jnp.where(left, pair[0:n, :], pair[n:, :])


def window_values(pair, beside, far):
    left = is_left()
    n = far.shape[0]
    return jnp.concatenate(
        [
            jnp.where(left, beside[0:n, :], far[...]),
            jnp.where(left, beside[n:, :], pair[0:n, :]),
            jnp.where(left, pair[0:n, :], pair[n:, :]),
            jnp.where(left, pair[n:, :], beside[0:n, :]),
            jnp.where(left, far[...], beside[n:, :]),
        ]
    )


def apply_out(turned, pair, near, far, local):
    return local[...] + dot(turned[...], window_values(pair, near, far))


def middle_kernel(
    turned, pair, near, far, local, state, prev, mass, send, returned, own, edge, message
):
    face = send.shape[1]
    total = apply_out(turned, pair, near, far, local)
    returned[...] = total[0:face, :].astype(BF16)
    own[...] = total[face:, :]
    m = widen(column(mass[...]), state.shape[1])
    current = state[...].astype(F32)
    partial = filter_scale * (m * own[...] - filter_shift * current) - prev[...].astype(F32)
    edge[...] = dot(hot_rows(send[...], state.shape[0]), (m * partial).astype(BF16)).astype(BF16)
    left = is_left()
    message[0] = jnp.where(left, edge[...], returned[...])
    message[1] = jnp.where(left, returned[...], edge[...])


def next_kernel(
    own, inner, outer, returned, ghost, state, prev, mass, send, table,
    first, scaled, ghost_next, sent, outward, base, field,
):
    face = send.shape[1]
    m = widen(column(mass[...]), state.shape[1])
    left = is_left()
    within = jnp.where(left, inner[1], inner[0])
    received = jnp.where(left, within, outer[...])
    edge = jnp.where(left, outer[...], within)
    owned = own[...] + dot(hot_columns(send[...], state.shape[0]), received)
    current = state[...].astype(F32)
    one = filter_scale * (m * owned - filter_shift * current) - prev[...].astype(F32)
    first[...] = one.astype(BF16)
    scaled[...] = (m * first[...].astype(F32)).astype(BF16)
    split = ghost[face : face + 16, :].astype(F32)
    g = widen(column(split[0:1, :] + split[1:2, :] + split[2:3, :]), state.shape[1])
    ghost_next[...] = (
        edge.astype(F32) + (filter_scale * g * g) * returned[...].astype(F32)
    ).astype(BF16)
    field[0:face, :] = ghost_next[...]
    field[face:, :] = scaled[...]
    store_sums(table, field, sent, outward, base)


def end_kernel(turned, pair, near, far, local, returned, own):
    face = returned.shape[0]
    total = apply_out(turned, pair, near, far, local)
    returned[...] = total[0:face, :].astype(BF16)
    own[...] = total[face:, :]


def last_kernel(own, received, state, first, mass, send, second):
    m = widen(column(mass[...]), state.shape[1])
    owned = own[...] + dot(hot_columns(send[...], state.shape[0]), received[...])
    two = filter_scale * (m * owned - filter_shift * first[...].astype(F32))
    second[...] = (two - state[...].astype(F32)).astype(BF16)


def call(kernel, outs, args, specs=None, scratch=(), mib=8):
    return pl.pallas_call(
        kernel,
        out_shape=[
            kept[0](*kept[1:]) if kept else jax.ShapeDtypeStruct(shape, kind)
            for shape, kind, *kept in outs
        ],
        in_specs=specs or [VMEM] * len(args),
        out_specs=[VMEM] * len(outs),
        scratch_shapes=list(scratch),
        compiler_params=pltpu.CompilerParams(vmem_limit_bytes=mib << 20),
    )(*args)


def kept(shape, kind):
    return (shape, kind, pltpu.VMEM, shape, kind)


def hold(block):
    return pltpu.with_memory_space_constraint(block, pltpu.VMEM)


def leave(block):
    return pltpu.with_memory_space_constraint(block, pltpu.HBM)


def inner_pairs(block):
    n = lax.axis_size("mesh")
    groups = [[i, i + 1] for i in range(0, n, 2)]
    return lax.all_gather(block, "mesh", axis=0, axis_index_groups=groups)


def outer_swap(block):
    n = lax.axis_size("mesh")
    route = [(i, i + 1 if i % 2 else i - 1) for i in range(1, n - 1)]
    return lax.ppermute(block, "mesh", route)


def two_away(block, way):
    n = lax.axis_size("mesh")
    route = [(i, i + (2 * way if i % 2 == 0 else -2 * way)) for i in range(n)]
    return lax.ppermute(block, "mesh", [(i, j) for i, j in route if 0 <= j < n])


def swap(block, axis, mask):
    return lax.ppermute(block, axis, [(i, i ^ mask) for i in range(lax.axis_size(axis))])


def shards(
    state,
    prev_state,
    mass,
    cell_nodes,
    cell_live,
    cell_scale,
    potential,
    stiffness,
    shape_values,
    cell_proj,
    cell_owner,
    cell_slot,
    coupling,
    send_rows,
):
    own_rows, orbitals = state.shape
    cells, per_cell = cell_nodes.shape
    atoms, per_atom = coupling.shape
    face = send_rows.shape[1]
    extended = own_rows + face
    block = atoms * per_atom
    window = 5 * block
    mass_row = mass.reshape(1, own_rows)
    other = swap(cell_proj, "band", 2)
    start = call
    scaled, outgoing, strengths = start(
        start_kernel,
        [
            ((own_rows, orbitals), BF16),
            ((face + 16, orbitals), BF16),
            ((16, orbitals), BF16),
        ],
        [leave(block) for block in (state, mass_row, send_rows, coupling)],
    )
    ghost = from_behind(outgoing, "mesh", 1)

    (pick,) = call(pick_kernel, [kept((cells * per_cell, extended), BF16)], (leave(cell_nodes),))
    pick = hold(pick)
    near = jnp.stack([cell_proj, other])
    far = swap(near, "band", 6)
    (operator,) = call(
        operator_kernel,
        [kept((cells, per_cell, per_cell), BF16)],
        (leave(potential), leave(stiffness), leave(shape_values), cell_live, cell_scale),
        specs=[VMEM, VMEM, VMEM, SMEM, SMEM],
    )
    operator = hold(operator)
    projectors = lax.all_gather(
        jnp.concatenate([near, far], axis=0),
        "band",
        axis=0,
        axis_index_groups=[[0, 1], [2, 3], [4, 5], [6, 7]],
    )

    sums_of = [((block, orbitals), BF16), ((2 * block, orbitals), BF16), ((2 * block, orbitals), F32)]
    table, *sums = call(
        table_kernel,
        [kept((window, extended), BF16)] + sums_of,
        (projectors, pick, cell_owner, cell_slot, cell_live, ghost, scaled),
        specs=[VMEM, VMEM, SMEM, SMEM, SMEM, VMEM, VMEM],
        scratch=[
            pltpu.VMEM((window, extended), F32),
            pltpu.VMEM((extended, orbitals), BF16),
            pltpu.VMEM((per_cell, block), F32),
        ],
    )
    table = hold(table)
    (turned,) = call(turn_kernel, [kept((extended, window), BF16)], (table,))
    turned = hold(turned)
    (place,) = call(place_kernel, [kept((extended, cells * per_cell), BF16)], (cell_nodes,))
    place = hold(place)

    def atom_values(sums, terms):
        sent, outward, base = sums
        far = two_away(sent, 1)
        near = outer_swap(outward)
        mine, message = call(
            join_kernel,
            [((2 * block, orbitals), F32), ((2 * block + 16, orbitals), BF16)],
            (base, near, far, strengths),
        )
        both = inner_pairs(message)
        pair, sent = call(
            couple_kernel,
            [((2 * block, orbitals), BF16), ((block, orbitals), BF16)],
            (mine, both, strengths),
        )
        far = two_away(sent, -1)
        near = outer_swap(pair)
        (local,) = call(scatter_kernel, [((extended, orbitals), F32)], (place, terms))
        return (pair, near, far), local

    def cell_terms(ghost, scaled):
        (terms,) = call(
            gather_kernel,
            [((cells * per_cell, orbitals), BF16)],
            (pick, operator, ghost, scaled),
            scratch=[
                pltpu.VMEM((extended, orbitals), BF16),
                pltpu.VMEM((cells * per_cell, orbitals), BF16),
            ],
        )
        return terms

    nodal = ((own_rows, orbitals), BF16)
    shared = ((face, orbitals), BF16)
    own_wide = ((own_rows, orbitals), F32)

    values, local = atom_values(sums, cell_terms(ghost, scaled))
    returned, own, _, message = call(
        middle_kernel,
        [shared, own_wide, shared, ((2, face, orbitals), BF16)],
        (turned, *values, local, state, prev_state, mass_row, send_rows),
    )
    outer = outer_swap(message[1])
    inner = inner_pairs(message[0])
    first, scaled_one, ghost_one, *sums_one = call(
        next_kernel,
        [nodal, nodal, shared] + sums_of,
        (own, inner, outer, returned, ghost, state, prev_state, mass_row, send_rows, table),
        scratch=[pltpu.VMEM((extended, orbitals), BF16)],
    )
    terms_one = cell_terms(ghost_one, scaled_one)
    values_one, local_one = atom_values(sums_one, terms_one)
    returned_one, own_one = call(
        end_kernel, [shared, own_wide], (turned, *values_one, local_one)
    )
    received_one = from_behind(returned_one, "mesh", -1)
    (second,) = call(
        last_kernel, [nodal], (own_one, received_one, state, first, mass_row, send_rows)
    )
    return (first, second)


def solution(mesh):
    placed = (
        P("mesh", "band"),
        P("mesh", "band"),
        P("mesh"),
        P("mesh", None),
        P("mesh"),
        P("mesh"),
        P("mesh", None),
        P(),
        P(),
        P("mesh", "band", None),
        P("mesh", None),
        P("mesh", None),
        P("mesh", None),
        P("mesh", None),
    )

    return jax.shard_map(
        shards,
        mesh=mesh,
        in_specs=placed,
        out_specs=(P("mesh", "band"), P("mesh", "band")),
        check_vma=False,
    )
```

```python
import jax
import jax.numpy as jnp
from jax import lax
from jax.experimental import pallas as pl
from jax.experimental.pallas import tpu as pltpu
from jax.sharding import PartitionSpec as P


APC = 8
FLIPS = (0, 1, 3, 2)
F32 = jnp.float32
BF16 = jnp.bfloat16
LANES = 128

filter_scale = 0.6
filter_shift = 1.0

VMEM = pl.BlockSpec(memory_space=pltpu.VMEM)
SMEM = pl.BlockSpec(memory_space=pltpu.SMEM)


def from_behind(block, axis, distance):
    devices = range(lax.axis_size(axis))
    route = [(i - distance, i) for i in devices if i - distance in devices]
    return lax.ppermute(block, axis, route)


def dot(a, b):
    return jnp.dot(a, b, preferred_element_type=F32)


def column(row):
    n = row.shape[1]
    parts = [
        jnp.transpose(jnp.broadcast_to(row[:, i : i + LANES], (LANES, LANES)))
        for i in range(0, n, LANES)
    ]
    return jnp.concatenate(parts, axis=0)


def widen(col, width):
    return jnp.concatenate([col] * (width // LANES), axis=1)


def hot_rows(row, width):
    col = column(row.astype(F32)).astype(jnp.int32)
    lane = lax.broadcasted_iota(jnp.int32, col.shape, 1)
    parts = [(col == lane + i).astype(F32).astype(BF16) for i in range(0, width, LANES)]
    return jnp.concatenate(parts, axis=1)


def hot_columns(row, height):
    n = row.shape[1]
    line = lax.broadcasted_iota(jnp.int32, (height, n), 0)
    return (line == row).astype(F32).astype(BF16)


def split_rows(row):
    high = row.astype(BF16).astype(F32)
    middle = (row - high).astype(BF16).astype(F32)
    low = row - high - middle
    line = lax.broadcasted_iota(jnp.int32, (16, row.shape[1]), 0)
    parts = jnp.where(line == 0, high, jnp.where(line == 1, middle, jnp.where(line == 2, low, 0.0)))
    return parts.astype(BF16)


def is_left():
    return lax.rem(lax.axis_index("mesh"), 2) == 0


def start_kernel(
    state, mass, send, coupling, projectors, scaled, outgoing, strengths, kept_projectors
):
    kept_projectors[...] = projectors[...]
    atoms, per_atom = coupling.shape
    width = atoms * per_atom
    spread = jnp.concatenate(
        [jnp.broadcast_to(coupling[a : a + 1, :], (per_atom, per_atom)) for a in range(atoms)], axis=0
    )
    line = lax.broadcasted_iota(jnp.int32, spread.shape, 0)
    lane = lax.broadcasted_iota(jnp.int32, spread.shape, 1)
    tall = jnp.sum(jnp.where(line % per_atom == lane, spread, 0.0), axis=1, keepdims=True)
    square = (width, width)
    diagonal = lax.broadcasted_iota(jnp.int32, square, 0) == lax.broadcasted_iota(jnp.int32, square, 1)
    row = jnp.sum(jnp.where(diagonal, jnp.broadcast_to(tall, square), 0.0), axis=0, keepdims=True)
    strengths[...] = jnp.concatenate([split_rows(row)] * (strengths.shape[1] // width), axis=1)
    m = widen(column(mass[...]), state.shape[1])
    scaled[...] = (m * state[...].astype(F32)).astype(BF16)
    face = send.shape[1]
    outgoing[0:face, :] = dot(hot_rows(send[...], state.shape[0]), scaled[...]).astype(BF16)
    outgoing[face : face + 16, :] = dot(
        split_rows(mass[...]), hot_columns(send[...], state.shape[0])
    ).astype(BF16)


def pick_kernel(nodes, pick):
    cells, per_cell = nodes.shape
    for c in range(cells):
        row = nodes[c : c + 1, :]
        pick[c * per_cell : (c + 1) * per_cell, :] = hot_rows(row, pick.shape[1])


def place_kernel(nodes, send, place, send_pick, send_place):
    send_pick[...] = hot_rows(send[...], send_pick.shape[1])
    send_place[...] = hot_columns(send[...], send_place.shape[0])
    cells, per_cell = nodes.shape
    for c in range(cells):
        row = nodes[c : c + 1, :]
        place[:, c * per_cell : (c + 1) * per_cell] = hot_columns(row, place.shape[0])


def operator_kernel(potential, stiffness, shape_values, live, scale, operator):
    values = shape_values[...].astype(F32)
    turned = jnp.transpose(shape_values[...])
    for c in range(potential.shape[0]):
        points = column(potential[c : c + 1, :])
        weighted = (widen(points, values.shape[1]) * values).astype(BF16)
        alive = jnp.where(c < live[0], 1.0, 0.0)
        local = 0.5 * scale[c] * stiffness[...].astype(F32) + dot(turned, weighted)
        operator[c] = (alive * local).astype(BF16)


def store_sums(table, field, sent, outward, base):
    sums = dot(table[...], field[...])
    n = sent.shape[0]
    left = is_left()
    sent[...] = jnp.where(left, sums[4 * n :, :], sums[0:n, :]).astype(BF16)
    outward[...] = jnp.where(left, sums[0 : 2 * n, :], sums[3 * n :, :]).astype(BF16)
    base[...] = jnp.where(left, sums[2 * n : 4 * n, :], sums[n : 3 * n, :])


def table_kernel(
    projectors, pick, owner, slot, live, ghost, scaled,
    table, sent, outward, base, wide, field, nodes,
):
    here, x = lax.axis_index("mesh"), lax.axis_index("band") // 2
    cells, per_atom = owner.shape[0], table.shape[0] // (5 * APC)
    per_cell = pick.shape[0] // cells
    share = projectors.shape[3]
    face = scaled.shape[0] // 4
    wide[...] = jnp.zeros_like(wide)
    field[0:face, :] = ghost[0:face, :]
    field[face:, :] = scaled[...]
    for c in range(cells):
        for i, flip in enumerate(FLIPS):
            for core in range(2):
                band = (x ^ flip) * 2 + core
                rows = pl.ds(pl.multiple_of(band * share, share), share)
                nodes[rows, :] = projectors[core, i, c].astype(F32)
        block = jnp.transpose(nodes[...]).astype(BF16)
        at_nodes = dot(block, pick[c * per_cell : (c + 1) * per_cell, :])
        at_nodes = at_nodes * jnp.where(c < live[0], 1.0, 0.0)
        for j in range(APC):
            target = (owner[c, j] - here + 2) * APC + slot[c, j]
            rows = pl.ds(pl.multiple_of(target * per_atom, per_atom), per_atom)
            wide[rows, :] = wide[rows, :] + at_nodes[per_atom * j : per_atom * (j + 1), :]
    table[...] = wide[...].astype(BF16)
    store_sums(table, field, sent, outward, base)


def turn_kernel(table, turned):
    turned[...] = jnp.transpose(table[...])


def gather_kernel(pick, operator, ghost, scaled, terms, field, held):
    face = scaled.shape[0] // 4
    cells, per_cell = operator.shape[0], operator.shape[1]
    field[0:face, :] = ghost[0:face, :]
    field[face:, :] = scaled[...]
    held[...] = dot(pick[...], field[...]).astype(BF16)
    for c in range(cells):
        rows = slice(c * per_cell, (c + 1) * per_cell)
        terms[rows, :] = dot(operator[c], held[rows, :]).astype(BF16)


def scatter_kernel(place, terms, out):
    out[...] = dot(place[...], terms[...])


def join_kernel(base, near, far, strengths, mine, message):
    n = far.shape[0]
    left = is_left()
    total = base[...] + near[...].astype(F32)
    added = far[...].astype(F32)
    mine[0:n, :] = total[0:n, :] + jnp.where(left, added, 0.0)
    mine[n:, :] = total[n:, :] + jnp.where(left, 0.0, added)
    message[0 : 2 * n, :] = mine[...].astype(BF16)
    message[2 * n :, :] = strengths[...]


def couple_kernel(mine, both, strengths, pair, sent):
    n = sent.shape[0]

    def tall(split):
        split = split.astype(F32)
        return column(split[0:1, 0:n] + split[1:2, 0:n] + split[2:3, 0:n])

    message = jnp.where(is_left(), both[1], both[0]).astype(F32)
    own, other = tall(strengths[...]), tall(message[2 * n :, :])
    left = is_left()
    for i in range(2):
        at = slice(i * n, (i + 1) * n)
        total = mine[at, :] + message[at, :]
        factor = jnp.where(left, own, other) if i == 0 else jnp.where(left, other, own)
        pair[at, :] = (widen(factor, total.shape[1]) * total).astype(BF16)
    sent[...] = jnp.where(left, pair[0:n, :], pair[n:, :])


def window_values(pair, beside, far):
    left = is_left()
    n = far.shape[0]
    return jnp.concatenate(
        [
            jnp.where(left, beside[0:n, :], far[...]),
            jnp.where(left, beside[n:, :], pair[0:n, :]),
            jnp.where(left, pair[0:n, :], pair[n:, :]),
            jnp.where(left, pair[n:, :], beside[0:n, :]),
            jnp.where(left, far[...], beside[n:, :]),
        ]
    )


def apply_out(turned, pair, near, far, local):
    return local[...] + dot(turned[...], window_values(pair, near, far))


def middle_kernel(
    turned, pair, near, far, local, state, prev, mass, send_pick, returned, own, edge, message
):
    face = send_pick.shape[0]
    total = apply_out(turned, pair, near, far, local)
    returned[...] = total[0:face, :].astype(BF16)
    own[...] = total[face:, :]
    m = widen(column(mass[...]), state.shape[1])
    current = state[...].astype(F32)
    partial = filter_scale * (m * own[...] - filter_shift * current) - prev[...].astype(F32)
    edge[...] = dot(send_pick[...], (m * partial).astype(BF16)).astype(BF16)
    left = is_left()
    message[0] = jnp.where(left, edge[...], returned[...])
    message[1] = jnp.where(left, returned[...], edge[...])


def next_kernel(
    own, inner, outer, returned, ghost, state, prev, mass, send_place, table,
    first, scaled, ghost_next, sent, outward, base, field,
):
    face = send_place.shape[1]
    m = widen(column(mass[...]), state.shape[1])
    left = is_left()
    within = jnp.where(left, inner[1], inner[0])
    received = jnp.where(left, within, outer[...])
    edge = jnp.where(left, outer[...], within)
    owned = own[...] + dot(send_place[...], received)
    current = state[...].astype(F32)
    one = filter_scale * (m * owned - filter_shift * current) - prev[...].astype(F32)
    first[...] = one.astype(BF16)
    scaled[...] = (m * first[...].astype(F32)).astype(BF16)
    split = ghost[face : face + 16, :].astype(F32)
    g = widen(column(split[0:1, :] + split[1:2, :] + split[2:3, :]), state.shape[1])
    ghost_next[...] = (
        edge.astype(F32) + (filter_scale * g * g) * returned[...].astype(F32)
    ).astype(BF16)
    field[0:face, :] = ghost_next[...]
    field[face:, :] = scaled[...]
    store_sums(table, field, sent, outward, base)


def end_kernel(turned, pair, near, far, local, returned, own):
    face = returned.shape[0]
    total = apply_out(turned, pair, near, far, local)
    returned[...] = total[0:face, :].astype(BF16)
    own[...] = total[face:, :]


def last_kernel(own, received, state, first, mass, send_place, second):
    m = widen(column(mass[...]), state.shape[1])
    owned = own[...] + dot(send_place[...], received[...])
    two = filter_scale * (m * owned - filter_shift * first[...].astype(F32))
    second[...] = (two - state[...].astype(F32)).astype(BF16)


def call(kernel, outs, args, specs=None, scratch=(), mib=8):
    return pl.pallas_call(
        kernel,
        out_shape=[
            kept[0](*kept[1:]) if kept else jax.ShapeDtypeStruct(shape, kind)
            for shape, kind, *kept in outs
        ],
        in_specs=specs or [VMEM] * len(args),
        out_specs=[VMEM] * len(outs),
        scratch_shapes=list(scratch),
        compiler_params=pltpu.CompilerParams(vmem_limit_bytes=mib << 20),
    )(*args)


def kept(shape, kind):
    return (shape, kind, pltpu.VMEM, shape, kind)


def hold(block):
    return pltpu.with_memory_space_constraint(block, pltpu.VMEM)


def leave(block):
    return pltpu.with_memory_space_constraint(block, pltpu.HBM)


def inner_pairs(block):
    n = lax.axis_size("mesh")
    groups = [[i, i + 1] for i in range(0, n, 2)]
    return lax.all_gather(block, "mesh", axis=0, axis_index_groups=groups)


def outer_swap(block):
    n = lax.axis_size("mesh")
    route = [(i, i + 1 if i % 2 else i - 1) for i in range(1, n - 1)]
    return lax.ppermute(block, "mesh", route)


def two_away(block, way):
    n = lax.axis_size("mesh")
    route = [(i, i + (2 * way if i % 2 == 0 else -2 * way)) for i in range(n)]
    return lax.ppermute(block, "mesh", [(i, j) for i, j in route if 0 <= j < n])


def swap(block, axis, mask):
    return lax.ppermute(block, axis, [(i, i ^ mask) for i in range(lax.axis_size(axis))])


def shards(
    state,
    prev_state,
    mass,
    cell_nodes,
    cell_live,
    cell_scale,
    potential,
    stiffness,
    shape_values,
    cell_proj,
    cell_owner,
    cell_slot,
    coupling,
    send_rows,
):
    own_rows, orbitals = state.shape
    cells, per_cell = cell_nodes.shape
    atoms, per_atom = coupling.shape
    face = send_rows.shape[1]
    extended = own_rows + face
    block = atoms * per_atom
    window = 5 * block
    mass_row = mass.reshape(1, own_rows)
    start = call
    scaled, outgoing, strengths, own_proj = start(
        start_kernel,
        [
            ((own_rows, orbitals), BF16),
            ((face + 16, orbitals), BF16),
            ((16, orbitals), BF16),
            (cell_proj.shape, BF16),
        ],
        [leave(block) for block in (state, mass_row, send_rows, coupling, cell_proj)],
    )
    other = swap(own_proj, "band", 2)
    ghost = from_behind(outgoing, "mesh", 1)

    (pick,) = call(pick_kernel, [kept((cells * per_cell, extended), BF16)], (leave(cell_nodes),))
    pick = hold(pick)
    near = jnp.stack([own_proj, other])
    far = swap(near, "band", 6)
    (operator,) = call(
        operator_kernel,
        [kept((cells, per_cell, per_cell), BF16)],
        (leave(potential), leave(stiffness), leave(shape_values), cell_live, cell_scale),
        specs=[VMEM, VMEM, VMEM, SMEM, SMEM],
    )
    operator = hold(operator)
    projectors = lax.all_gather(
        jnp.concatenate([near, far], axis=0),
        "band",
        axis=0,
        axis_index_groups=[[0, 1], [2, 3], [4, 5], [6, 7]],
    )

    sums_of = [((block, orbitals), BF16), ((2 * block, orbitals), BF16), ((2 * block, orbitals), F32)]
    table, *sums = call(
        table_kernel,
        [kept((window, extended), BF16)] + sums_of,
        (projectors, pick, cell_owner, cell_slot, cell_live, ghost, scaled),
        specs=[VMEM, VMEM, SMEM, SMEM, SMEM, VMEM, VMEM],
        scratch=[
            pltpu.VMEM((window, extended), F32),
            pltpu.VMEM((extended, orbitals), BF16),
            pltpu.VMEM((per_cell, block), F32),
        ],
    )
    table = hold(table)
    (turned,) = call(turn_kernel, [kept((extended, window), BF16)], (table,))
    turned = hold(turned)
    place, send_pick, send_place = call(
        place_kernel,
        [
            kept((extended, cells * per_cell), BF16),
            kept((face, own_rows), BF16),
            kept((own_rows, face), BF16),
        ],
        (cell_nodes, send_rows),
    )
    place, send_pick, send_place = hold(place), hold(send_pick), hold(send_place)

    def atom_values(sums, terms):
        sent, outward, base = sums
        far = two_away(sent, 1)
        near = outer_swap(outward)
        mine, message = call(
            join_kernel,
            [((2 * block, orbitals), F32), ((2 * block + 16, orbitals), BF16)],
            (base, near, far, strengths),
        )
        both = inner_pairs(message)
        pair, sent = call(
            couple_kernel,
            [((2 * block, orbitals), BF16), ((block, orbitals), BF16)],
            (mine, both, strengths),
        )
        far = two_away(sent, -1)
        near = outer_swap(pair)
        (local,) = call(scatter_kernel, [((extended, orbitals), F32)], (place, terms))
        return (pair, near, far), local

    def cell_terms(ghost, scaled):
        (terms,) = call(
            gather_kernel,
            [((cells * per_cell, orbitals), BF16)],
            (pick, operator, ghost, scaled),
            scratch=[
                pltpu.VMEM((extended, orbitals), BF16),
                pltpu.VMEM((cells * per_cell, orbitals), BF16),
            ],
        )
        return terms

    nodal = ((own_rows, orbitals), BF16)
    shared = ((face, orbitals), BF16)
    own_wide = ((own_rows, orbitals), F32)

    values, local = atom_values(sums, cell_terms(ghost, scaled))
    returned, own, _, message = call(
        middle_kernel,
        [shared, own_wide, shared, ((2, face, orbitals), BF16)],
        (turned, *values, local, state, prev_state, mass_row, send_pick),
    )
    outer = outer_swap(message[1])
    inner = inner_pairs(message[0])
    first, scaled_one, ghost_one, *sums_one = call(
        next_kernel,
        [nodal, nodal, shared] + sums_of,
        (own, inner, outer, returned, ghost, state, prev_state, mass_row, send_place, table),
        scratch=[pltpu.VMEM((extended, orbitals), BF16)],
    )
    terms_one = cell_terms(ghost_one, scaled_one)
    values_one, local_one = atom_values(sums_one, terms_one)
    returned_one, own_one = call(
        end_kernel, [shared, own_wide], (turned, *values_one, local_one)
    )
    received_one = from_behind(returned_one, "mesh", -1)
    (second,) = call(
        last_kernel, [nodal], (own_one, received_one, state, first, mass_row, send_place)
    )
    return (first, second)


def solution(mesh):
    placed = (
        P("mesh", "band"),
        P("mesh", "band"),
        P("mesh"),
        P("mesh", None),
        P("mesh"),
        P("mesh"),
        P("mesh", None),
        P(),
        P(),
        P("mesh", "band", None),
        P("mesh", None),
        P("mesh", None),
        P("mesh", None),
        P("mesh", None),
    )

    return jax.shard_map(
        shards,
        mesh=mesh,
        in_specs=placed,
        out_specs=(P("mesh", "band"), P("mesh", "band")),
        check_vma=False,
    )
```

```python
import jax
import jax.numpy as jnp
from jax import lax
from jax.experimental import pallas as pl
from jax.experimental.pallas import tpu as pltpu
from jax.sharding import PartitionSpec as P


APC = 8
FLIPS = (0, 1, 3, 2)
F32 = jnp.float32
BF16 = jnp.bfloat16
LANES = 128

filter_scale = 0.6
filter_shift = 1.0

VMEM = pl.BlockSpec(memory_space=pltpu.VMEM)
SMEM = pl.BlockSpec(memory_space=pltpu.SMEM)


def from_behind(block, axis, distance):
    devices = range(lax.axis_size(axis))
    route = [(i - distance, i) for i in devices if i - distance in devices]
    return lax.ppermute(block, axis, route)


def dot(a, b):
    return jnp.dot(a, b, preferred_element_type=F32)


def column(row):
    n = row.shape[1]
    parts = [
        jnp.transpose(jnp.broadcast_to(row[:, i : i + LANES], (LANES, LANES)))
        for i in range(0, n, LANES)
    ]
    return jnp.concatenate(parts, axis=0)


def widen(col, width):
    return jnp.concatenate([col] * (width // LANES), axis=1)


def hot_rows(row, width):
    col = column(row.astype(F32)).astype(jnp.int32)
    lane = lax.broadcasted_iota(jnp.int32, col.shape, 1)
    parts = [(col == lane + i).astype(F32).astype(BF16) for i in range(0, width, LANES)]
    return jnp.concatenate(parts, axis=1)


def hot_columns(row, height):
    n = row.shape[1]
    line = lax.broadcasted_iota(jnp.int32, (height, n), 0)
    return (line == row).astype(F32).astype(BF16)


def split_rows(row):
    high = row.astype(BF16).astype(F32)
    middle = (row - high).astype(BF16).astype(F32)
    low = row - high - middle
    line = lax.broadcasted_iota(jnp.int32, (16, row.shape[1]), 0)
    parts = jnp.where(line == 0, high, jnp.where(line == 1, middle, jnp.where(line == 2, low, 0.0)))
    return parts.astype(BF16)


def is_left():
    return lax.rem(lax.axis_index("mesh"), 2) == 0


def start_kernel(
    state, mass, send, coupling, projectors, scaled, outgoing, strengths, kept_projectors
):
    kept_projectors[...] = projectors[...]
    atoms, per_atom = coupling.shape
    width = atoms * per_atom
    spread = jnp.concatenate(
        [jnp.broadcast_to(coupling[a : a + 1, :], (per_atom, per_atom)) for a in range(atoms)], axis=0
    )
    line = lax.broadcasted_iota(jnp.int32, spread.shape, 0)
    lane = lax.broadcasted_iota(jnp.int32, spread.shape, 1)
    tall = jnp.sum(jnp.where(line % per_atom == lane, spread, 0.0), axis=1, keepdims=True)
    square = (width, width)
    diagonal = lax.broadcasted_iota(jnp.int32, square, 0) == lax.broadcasted_iota(jnp.int32, square, 1)
    row = jnp.sum(jnp.where(diagonal, jnp.broadcast_to(tall, square), 0.0), axis=0, keepdims=True)
    strengths[...] = jnp.concatenate([split_rows(row)] * (strengths.shape[1] // width), axis=1)
    m = widen(column(mass[...]), state.shape[1])
    scaled[...] = (m * state[...].astype(F32)).astype(BF16)
    face = send.shape[1]
    outgoing[0:face, :] = dot(hot_rows(send[...], state.shape[0]), scaled[...]).astype(BF16)
    outgoing[face : face + 16, :] = dot(
        split_rows(mass[...]), hot_columns(send[...], state.shape[0])
    ).astype(BF16)


def pick_kernel(nodes, pick):
    cells, per_cell = nodes.shape
    for c in range(cells):
        row = nodes[c : c + 1, :]
        pick[c * per_cell : (c + 1) * per_cell, :] = hot_rows(row, pick.shape[1])


def place_kernel(nodes, send, place, send_pick, send_place):
    send_pick[...] = hot_rows(send[...], send_pick.shape[1])
    send_place[...] = hot_columns(send[...], send_place.shape[0])
    cells, per_cell = nodes.shape
    for c in range(cells):
        row = nodes[c : c + 1, :]
        place[:, c * per_cell : (c + 1) * per_cell] = hot_columns(row, place.shape[0])


def operator_kernel(potential, stiffness, shape_values, live, scale, operator):
    values = shape_values[...].astype(F32)
    turned = jnp.transpose(shape_values[...])
    for c in range(potential.shape[0]):
        points = column(potential[c : c + 1, :])
        weighted = (widen(points, values.shape[1]) * values).astype(BF16)
        alive = jnp.where(c < live[0], 1.0, 0.0)
        local = 0.5 * scale[c] * stiffness[...].astype(F32) + dot(turned, weighted)
        operator[c] = (alive * local).astype(BF16)


def store_sums(table, field, sent, outward, base):
    sums = dot(table[...], field[...])
    n = sent.shape[0]
    left = is_left()
    sent[...] = jnp.where(left, sums[4 * n :, :], sums[0:n, :]).astype(BF16)
    outward[...] = jnp.where(left, sums[0 : 2 * n, :], sums[3 * n :, :]).astype(BF16)
    base[...] = jnp.where(left, sums[2 * n : 4 * n, :], sums[n : 3 * n, :])


def table_kernel(
    projectors, pick, owner, slot, live, ghost, scaled,
    table, sent, outward, base, wide, field, nodes,
):
    here, x = lax.axis_index("mesh"), lax.axis_index("band") // 2
    cells, per_atom = owner.shape[0], table.shape[0] // (5 * APC)
    per_cell = pick.shape[0] // cells
    share = projectors.shape[3]
    face = scaled.shape[0] // 4
    wide[...] = jnp.zeros_like(wide)
    field[0:face, :] = ghost[0:face, :]
    field[face:, :] = scaled[...]
    for c in range(cells):
        for i, flip in enumerate(FLIPS):
            for core in range(2):
                band = (x ^ flip) * 2 + core
                rows = pl.ds(pl.multiple_of(band * share, share), share)
                nodes[rows, :] = projectors[core, i, c]
        block = jnp.transpose(nodes[...])
        at_nodes = dot(block, pick[c * per_cell : (c + 1) * per_cell, :])
        at_nodes = at_nodes * jnp.where(c < live[0], 1.0, 0.0)
        for j in range(APC):
            target = (owner[c, j] - here + 2) * APC + slot[c, j]
            rows = pl.ds(pl.multiple_of(target * per_atom, per_atom), per_atom)
            wide[rows, :] = wide[rows, :] + at_nodes[per_atom * j : per_atom * (j + 1), :]
    table[...] = wide[...].astype(BF16)
    store_sums(table, field, sent, outward, base)


def turn_kernel(table, turned):
    turned[...] = jnp.transpose(table[...])


def gather_kernel(pick, operator, ghost, scaled, terms, field, held):
    face = scaled.shape[0] // 4
    cells, per_cell = operator.shape[0], operator.shape[1]
    field[0:face, :] = ghost[0:face, :]
    field[face:, :] = scaled[...]
    held[...] = dot(pick[...], field[...]).astype(BF16)
    for c in range(cells):
        rows = slice(c * per_cell, (c + 1) * per_cell)
        terms[rows, :] = dot(operator[c], held[rows, :]).astype(BF16)


def scatter_kernel(place, terms, out):
    out[...] = dot(place[...], terms[...])


def join_kernel(base, near, far, strengths, mine, message):
    n = far.shape[0]
    left = is_left()
    total = base[...] + near[...].astype(F32)
    added = far[...].astype(F32)
    mine[0:n, :] = total[0:n, :] + jnp.where(left, added, 0.0)
    mine[n:, :] = total[n:, :] + jnp.where(left, 0.0, added)
    message[0 : 2 * n, :] = mine[...].astype(BF16)
    message[2 * n :, :] = strengths[...]


def couple_kernel(mine, both, strengths, pair, sent):
    n = sent.shape[0]

    def tall(split):
        split = split.astype(F32)
        return column(split[0:1, 0:n] + split[1:2, 0:n] + split[2:3, 0:n])

    message = jnp.where(is_left(), both[1], both[0]).astype(F32)
    own, other = tall(strengths[...]), tall(message[2 * n :, :])
    left = is_left()
    for i in range(2):
        at = slice(i * n, (i + 1) * n)
        total = mine[at, :] + message[at, :]
        factor = jnp.where(left, own, other) if i == 0 else jnp.where(left, other, own)
        pair[at, :] = (widen(factor, total.shape[1]) * total).astype(BF16)
    sent[...] = jnp.where(left, pair[0:n, :], pair[n:, :])


def window_values(pair, beside, far):
    left = is_left()
    n = far.shape[0]
    return jnp.concatenate(
        [
            jnp.where(left, beside[0:n, :], far[...]),
            jnp.where(left, beside[n:, :], pair[0:n, :]),
            jnp.where(left, pair[0:n, :], pair[n:, :]),
            jnp.where(left, pair[n:, :], beside[0:n, :]),
            jnp.where(left, far[...], beside[n:, :]),
        ]
    )


def apply_out(turned, pair, near, far, local):
    return local[...] + dot(turned[...], window_values(pair, near, far))


def middle_kernel(
    turned, pair, near, far, local, state, prev, mass, send_pick, returned, own, edge, message
):
    face = send_pick.shape[0]
    total = apply_out(turned, pair, near, far, local)
    returned[...] = total[0:face, :].astype(BF16)
    own[...] = total[face:, :]
    m = widen(column(mass[...]), state.shape[1])
    current = state[...].astype(F32)
    partial = filter_scale * (m * own[...] - filter_shift * current) - prev[...].astype(F32)
    edge[...] = dot(send_pick[...], (m * partial).astype(BF16)).astype(BF16)
    left = is_left()
    message[0] = jnp.where(left, edge[...], returned[...])
    message[1] = jnp.where(left, returned[...], edge[...])


def next_kernel(
    own, inner, outer, returned, ghost, state, prev, mass, send_place, table,
    first, scaled, ghost_next, sent, outward, base, field,
):
    face = send_place.shape[1]
    m = widen(column(mass[...]), state.shape[1])
    left = is_left()
    within = jnp.where(left, inner[1], inner[0])
    received = jnp.where(left, within, outer[...])
    edge = jnp.where(left, outer[...], within)
    owned = own[...] + dot(send_place[...], received)
    current = state[...].astype(F32)
    one = filter_scale * (m * owned - filter_shift * current) - prev[...].astype(F32)
    first[...] = one.astype(BF16)
    scaled[...] = (m * first[...].astype(F32)).astype(BF16)
    split = ghost[face : face + 16, :].astype(F32)
    g = widen(column(split[0:1, :] + split[1:2, :] + split[2:3, :]), state.shape[1])
    ghost_next[...] = (
        edge.astype(F32) + (filter_scale * g * g) * returned[...].astype(F32)
    ).astype(BF16)
    field[0:face, :] = ghost_next[...]
    field[face:, :] = scaled[...]
    store_sums(table, field, sent, outward, base)


def end_kernel(turned, pair, near, far, local, returned, own):
    face = returned.shape[0]
    total = apply_out(turned, pair, near, far, local)
    returned[...] = total[0:face, :].astype(BF16)
    own[...] = total[face:, :]


def last_kernel(own, received, state, first, mass, send_place, second):
    m = widen(column(mass[...]), state.shape[1])
    owned = own[...] + dot(send_place[...], received[...])
    two = filter_scale * (m * owned - filter_shift * first[...].astype(F32))
    second[...] = (two - state[...].astype(F32)).astype(BF16)


def call(kernel, outs, args, specs=None, scratch=(), mib=8):
    return pl.pallas_call(
        kernel,
        out_shape=[
            kept[0](*kept[1:]) if kept else jax.ShapeDtypeStruct(shape, kind)
            for shape, kind, *kept in outs
        ],
        in_specs=specs or [VMEM] * len(args),
        out_specs=[VMEM] * len(outs),
        scratch_shapes=list(scratch),
        compiler_params=pltpu.CompilerParams(vmem_limit_bytes=mib << 20),
    )(*args)


def kept(shape, kind):
    return (shape, kind, pltpu.VMEM, shape, kind)


def hold(block):
    return pltpu.with_memory_space_constraint(block, pltpu.VMEM)


def leave(block):
    return pltpu.with_memory_space_constraint(block, pltpu.HBM)


def inner_pairs(block):
    n = lax.axis_size("mesh")
    groups = [[i, i + 1] for i in range(0, n, 2)]
    return lax.all_gather(block, "mesh", axis=0, axis_index_groups=groups)


def outer_swap(block):
    n = lax.axis_size("mesh")
    route = [(i, i + 1 if i % 2 else i - 1) for i in range(1, n - 1)]
    return lax.ppermute(block, "mesh", route)


def two_away(block, way):
    n = lax.axis_size("mesh")
    route = [(i, i + (2 * way if i % 2 == 0 else -2 * way)) for i in range(n)]
    return lax.ppermute(block, "mesh", [(i, j) for i, j in route if 0 <= j < n])


def swap(block, axis, mask):
    return lax.ppermute(block, axis, [(i, i ^ mask) for i in range(lax.axis_size(axis))])


def shards(
    state,
    prev_state,
    mass,
    cell_nodes,
    cell_live,
    cell_scale,
    potential,
    stiffness,
    shape_values,
    cell_proj,
    cell_owner,
    cell_slot,
    coupling,
    send_rows,
):
    own_rows, orbitals = state.shape
    cells, per_cell = cell_nodes.shape
    atoms, per_atom = coupling.shape
    face = send_rows.shape[1]
    extended = own_rows + face
    block = atoms * per_atom
    window = 5 * block
    mass_row = mass.reshape(1, own_rows)
    start = call
    scaled, outgoing, strengths, own_proj = start(
        start_kernel,
        [
            ((own_rows, orbitals), BF16),
            ((face + 16, orbitals), BF16),
            ((16, orbitals), BF16),
            (cell_proj.shape, BF16),
        ],
        [leave(block) for block in (state, mass_row, send_rows, coupling, cell_proj)],
    )
    other = swap(cell_proj, "band", 2)
    ghost = from_behind(outgoing, "mesh", 1)

    (pick,) = call(pick_kernel, [kept((cells * per_cell, extended), BF16)], (leave(cell_nodes),))
    pick = hold(pick)
    near = jnp.stack([own_proj, other])
    far = swap(near, "band", 6)
    (operator,) = call(
        operator_kernel,
        [kept((cells, per_cell, per_cell), BF16)],
        (leave(potential), leave(stiffness), leave(shape_values), cell_live, cell_scale),
        specs=[VMEM, VMEM, VMEM, SMEM, SMEM],
    )
    operator = hold(operator)
    projectors = lax.all_gather(
        jnp.concatenate([near, far], axis=0),
        "band",
        axis=0,
        axis_index_groups=[[0, 1], [2, 3], [4, 5], [6, 7]],
    )

    sums_of = [((block, orbitals), BF16), ((2 * block, orbitals), BF16), ((2 * block, orbitals), F32)]
    table, *sums = call(
        table_kernel,
        [kept((window, extended), BF16)] + sums_of,
        (projectors, pick, cell_owner, cell_slot, cell_live, ghost, scaled),
        specs=[VMEM, VMEM, SMEM, SMEM, SMEM, VMEM, VMEM],
        scratch=[
            pltpu.VMEM((window, extended), F32),
            pltpu.VMEM((extended, orbitals), BF16),
            pltpu.VMEM((per_cell, block), BF16),
        ],
    )
    table = hold(table)
    (turned,) = call(turn_kernel, [kept((extended, window), BF16)], (table,))
    turned = hold(turned)
    place, send_pick, send_place = call(
        place_kernel,
        [
            kept((extended, cells * per_cell), BF16),
            kept((face, own_rows), BF16),
            kept((own_rows, face), BF16),
        ],
        (cell_nodes, send_rows),
    )
    place, send_pick, send_place = hold(place), hold(send_pick), hold(send_place)

    def atom_values(sums, terms):
        sent, outward, base = sums
        far = two_away(sent, 1)
        near = outer_swap(outward)
        mine, message = call(
            join_kernel,
            [((2 * block, orbitals), F32), ((2 * block + 16, orbitals), BF16)],
            (base, near, far, strengths),
        )
        both = inner_pairs(message)
        pair, sent = call(
            couple_kernel,
            [((2 * block, orbitals), BF16), ((block, orbitals), BF16)],
            (mine, both, strengths),
        )
        far = two_away(sent, -1)
        near = outer_swap(pair)
        (local,) = call(scatter_kernel, [((extended, orbitals), F32)], (place, terms))
        return (pair, near, far), local

    def cell_terms(ghost, scaled):
        (terms,) = call(
            gather_kernel,
            [((cells * per_cell, orbitals), BF16)],
            (pick, operator, ghost, scaled),
            scratch=[
                pltpu.VMEM((extended, orbitals), BF16),
                pltpu.VMEM((cells * per_cell, orbitals), BF16),
            ],
        )
        return terms

    nodal = ((own_rows, orbitals), BF16)
    shared = ((face, orbitals), BF16)
    own_wide = ((own_rows, orbitals), F32)

    values, local = atom_values(sums, cell_terms(ghost, scaled))
    returned, own, _, message = call(
        middle_kernel,
        [shared, own_wide, shared, ((2, face, orbitals), BF16)],
        (turned, *values, local, state, prev_state, mass_row, send_pick),
    )
    outer = outer_swap(message[1])
    inner = inner_pairs(message[0])
    first, scaled_one, ghost_one, *sums_one = call(
        next_kernel,
        [nodal, nodal, shared] + sums_of,
        (own, inner, outer, returned, ghost, state, prev_state, mass_row, send_place, table),
        scratch=[pltpu.VMEM((extended, orbitals), BF16)],
    )
    terms_one = cell_terms(ghost_one, scaled_one)
    values_one, local_one = atom_values(sums_one, terms_one)
    returned_one, own_one = call(
        end_kernel, [shared, own_wide], (turned, *values_one, local_one)
    )
    received_one = from_behind(returned_one, "mesh", -1)
    (second,) = call(
        last_kernel, [nodal], (own_one, received_one, state, first, mass_row, send_place)
    )
    return (first, second)


def solution(mesh):
    placed = (
        P("mesh", "band"),
        P("mesh", "band"),
        P("mesh"),
        P("mesh", None),
        P("mesh"),
        P("mesh"),
        P("mesh", None),
        P(),
        P(),
        P("mesh", "band", None),
        P("mesh", None),
        P("mesh", None),
        P("mesh", None),
        P("mesh", None),
    )

    return jax.shard_map(
        shards,
        mesh=mesh,
        in_specs=placed,
        out_specs=(P("mesh", "band"), P("mesh", "band")),
        check_vma=False,
    )
```

```python
import jax
import jax.numpy as jnp
from jax import lax
from jax.experimental import pallas as pl
from jax.experimental.pallas import tpu as pltpu
from jax.sharding import PartitionSpec as P


APC = 8
FLIPS = (0, 1, 3, 2)
F32 = jnp.float32
BF16 = jnp.bfloat16
LANES = 128

filter_scale = 0.6
filter_shift = 1.0

VMEM = pl.BlockSpec(memory_space=pltpu.VMEM)
SMEM = pl.BlockSpec(memory_space=pltpu.SMEM)


def from_behind(block, axis, distance):
    devices = range(lax.axis_size(axis))
    route = [(i - distance, i) for i in devices if i - distance in devices]
    return lax.ppermute(block, axis, route)


def dot(a, b):
    return jnp.dot(a, b, preferred_element_type=F32)


def column(row):
    n = row.shape[1]
    parts = [
        jnp.transpose(jnp.broadcast_to(row[:, i : i + LANES], (LANES, LANES)))
        for i in range(0, n, LANES)
    ]
    return jnp.concatenate(parts, axis=0)


def widen(col, width):
    return jnp.concatenate([col] * (width // LANES), axis=1)


def hot_rows(row, width):
    col = column(row.astype(F32)).astype(jnp.int32)
    lane = lax.broadcasted_iota(jnp.int32, col.shape, 1)
    parts = [(col == lane + i).astype(F32).astype(BF16) for i in range(0, width, LANES)]
    return jnp.concatenate(parts, axis=1)


def hot_columns(row, height):
    n = row.shape[1]
    line = lax.broadcasted_iota(jnp.int32, (height, n), 0)
    return (line == row).astype(F32).astype(BF16)


def split_rows(row):
    high = row.astype(BF16).astype(F32)
    middle = (row - high).astype(BF16).astype(F32)
    low = row - high - middle
    line = lax.broadcasted_iota(jnp.int32, (16, row.shape[1]), 0)
    parts = jnp.where(line == 0, high, jnp.where(line == 1, middle, jnp.where(line == 2, low, 0.0)))
    return parts.astype(BF16)


def is_left():
    return lax.rem(lax.axis_index("mesh"), 2) == 0


def start_kernel(
    state, mass, send, coupling, projectors, scaled, outgoing, strengths, kept_projectors
):
    kept_projectors[...] = projectors[...]
    atoms, per_atom = coupling.shape
    width = atoms * per_atom
    spread = jnp.concatenate(
        [jnp.broadcast_to(coupling[a : a + 1, :], (per_atom, per_atom)) for a in range(atoms)], axis=0
    )
    line = lax.broadcasted_iota(jnp.int32, spread.shape, 0)
    lane = lax.broadcasted_iota(jnp.int32, spread.shape, 1)
    tall = jnp.sum(jnp.where(line % per_atom == lane, spread, 0.0), axis=1, keepdims=True)
    square = (width, width)
    diagonal = lax.broadcasted_iota(jnp.int32, square, 0) == lax.broadcasted_iota(jnp.int32, square, 1)
    row = jnp.sum(jnp.where(diagonal, jnp.broadcast_to(tall, square), 0.0), axis=0, keepdims=True)
    strengths[...] = jnp.concatenate([split_rows(row)] * (strengths.shape[1] // width), axis=1)
    m = widen(column(mass[...]), state.shape[1])
    scaled[...] = (m * state[...].astype(F32)).astype(BF16)
    face = send.shape[1]
    outgoing[0:face, :] = dot(hot_rows(send[...], state.shape[0]), scaled[...]).astype(BF16)
    outgoing[face : face + 16, :] = dot(
        split_rows(mass[...]), hot_columns(send[...], state.shape[0])
    ).astype(BF16)


def pick_kernel(nodes, pick):
    cells, per_cell = nodes.shape
    for c in range(cells):
        row = nodes[c : c + 1, :]
        pick[c * per_cell : (c + 1) * per_cell, :] = hot_rows(row, pick.shape[1])


def place_kernel(nodes, place):
    cells, per_cell = nodes.shape
    for c in range(cells):
        row = nodes[c : c + 1, :]
        place[:, c * per_cell : (c + 1) * per_cell] = hot_columns(row, place.shape[0])


def operator_kernel(potential, stiffness, shape_values, live, scale, operator):
    values = shape_values[...].astype(F32)
    turned = jnp.transpose(shape_values[...])
    for c in range(potential.shape[0]):
        points = column(potential[c : c + 1, :])
        weighted = (widen(points, values.shape[1]) * values).astype(BF16)
        alive = jnp.where(c < live[0], 1.0, 0.0)
        local = 0.5 * scale[c] * stiffness[...].astype(F32) + dot(turned, weighted)
        operator[c] = (alive * local).astype(BF16)


def store_sums(table, field, sent, outward, base):
    sums = dot(table[...], field[...])
    n = sent.shape[0]
    left = is_left()
    sent[...] = jnp.where(left, sums[4 * n :, :], sums[0:n, :]).astype(BF16)
    outward[...] = jnp.where(left, sums[0 : 2 * n, :], sums[3 * n :, :]).astype(BF16)
    base[...] = jnp.where(left, sums[2 * n : 4 * n, :], sums[n : 3 * n, :])


def table_kernel(
    projectors, pick, owner, slot, live, ghost, scaled,
    table, sent, outward, base, wide, field, nodes,
):
    here, x = lax.axis_index("mesh"), lax.axis_index("band") // 2
    cells, per_atom = owner.shape[0], table.shape[0] // (5 * APC)
    per_cell = pick.shape[0] // cells
    share = projectors.shape[3]
    face = scaled.shape[0] // 4
    wide[...] = jnp.zeros_like(wide)
    field[0:face, :] = ghost[0:face, :]
    field[face:, :] = scaled[...]
    for c in range(cells):
        for i, flip in enumerate(FLIPS):
            for core in range(2):
                band = (x ^ flip) * 2 + core
                rows = pl.ds(pl.multiple_of(band * share, share), share)
                nodes[rows, :] = projectors[core, i, c]
        block = jnp.transpose(nodes[...])
        at_nodes = dot(block, pick[c * per_cell : (c + 1) * per_cell, :])
        at_nodes = at_nodes * jnp.where(c < live[0], 1.0, 0.0)
        for j in range(APC):
            target = (owner[c, j] - here + 2) * APC + slot[c, j]
            rows = pl.ds(pl.multiple_of(target * per_atom, per_atom), per_atom)
            wide[rows, :] = wide[rows, :] + at_nodes[per_atom * j : per_atom * (j + 1), :]
    table[...] = wide[...].astype(BF16)
    store_sums(table, field, sent, outward, base)


def turn_kernel(table, turned):
    turned[...] = jnp.transpose(table[...])


def gather_kernel(pick, operator, ghost, scaled, terms, field, held):
    face = scaled.shape[0] // 4
    cells, per_cell = operator.shape[0], operator.shape[1]
    field[0:face, :] = ghost[0:face, :]
    field[face:, :] = scaled[...]
    held[...] = dot(pick[...], field[...]).astype(BF16)
    for c in range(cells):
        rows = slice(c * per_cell, (c + 1) * per_cell)
        terms[rows, :] = dot(operator[c], held[rows, :]).astype(BF16)


def scatter_kernel(place, terms, out):
    out[...] = dot(place[...], terms[...])


def join_kernel(base, near, far, strengths, mine, message):
    n = far.shape[0]
    left = is_left()
    total = base[...] + near[...].astype(F32)
    added = far[...].astype(F32)
    mine[0:n, :] = total[0:n, :] + jnp.where(left, added, 0.0)
    mine[n:, :] = total[n:, :] + jnp.where(left, 0.0, added)
    message[0 : 2 * n, :] = mine[...].astype(BF16)
    message[2 * n :, :] = strengths[...]


def couple_kernel(mine, both, strengths, pair, sent):
    n = sent.shape[0]

    def tall(split):
        split = split.astype(F32)
        return column(split[0:1, 0:n] + split[1:2, 0:n] + split[2:3, 0:n])

    message = jnp.where(is_left(), both[1], both[0]).astype(F32)
    own, other = tall(strengths[...]), tall(message[2 * n :, :])
    left = is_left()
    for i in range(2):
        at = slice(i * n, (i + 1) * n)
        total = mine[at, :] + message[at, :]
        factor = jnp.where(left, own, other) if i == 0 else jnp.where(left, other, own)
        pair[at, :] = (widen(factor, total.shape[1]) * total).astype(BF16)
    sent[...] = jnp.where(left, pair[0:n, :], pair[n:, :])


def window_values(pair, beside, far):
    left = is_left()
    n = far.shape[0]
    return jnp.concatenate(
        [
            jnp.where(left, beside[0:n, :], far[...]),
            jnp.where(left, beside[n:, :], pair[0:n, :]),
            jnp.where(left, pair[0:n, :], pair[n:, :]),
            jnp.where(left, pair[n:, :], beside[0:n, :]),
            jnp.where(left, far[...], beside[n:, :]),
        ]
    )


def apply_out(turned, pair, near, far, local):
    return local[...] + dot(turned[...], window_values(pair, near, far))


def middle_kernel(
    turned, pair, near, far, local, state, prev, mass, send, returned, own, edge, message
):
    face = send.shape[1]
    total = apply_out(turned, pair, near, far, local)
    returned[...] = total[0:face, :].astype(BF16)
    own[...] = total[face:, :]
    m = widen(column(mass[...]), state.shape[1])
    current = state[...].astype(F32)
    partial = filter_scale * (m * own[...] - filter_shift * current) - prev[...].astype(F32)
    edge[...] = dot(hot_rows(send[...], state.shape[0]), (m * partial).astype(BF16)).astype(BF16)
    left = is_left()
    message[0] = jnp.where(left, edge[...], returned[...])
    message[1] = jnp.where(left, returned[...], edge[...])


def next_kernel(
    own, inner, outer, returned, ghost, state, prev, mass, send, table,
    first, scaled, ghost_next, sent, outward, base, field,
):
    face = send.shape[1]
    m = widen(column(mass[...]), state.shape[1])
    left = is_left()
    within = jnp.where(left, inner[1], inner[0])
    received = jnp.where(left, within, outer[...])
    edge = jnp.where(left, outer[...], within)
    owned = own[...] + dot(hot_columns(send[...], state.shape[0]), received)
    current = state[...].astype(F32)
    one = filter_scale * (m * owned - filter_shift * current) - prev[...].astype(F32)
    first[...] = one.astype(BF16)
    scaled[...] = (m * first[...].astype(F32)).astype(BF16)
    split = ghost[face : face + 16, :].astype(F32)
    g = widen(column(split[0:1, :] + split[1:2, :] + split[2:3, :]), state.shape[1])
    ghost_next[...] = (
        edge.astype(F32) + (filter_scale * g * g) * returned[...].astype(F32)
    ).astype(BF16)
    field[0:face, :] = ghost_next[...]
    field[face:, :] = scaled[...]
    store_sums(table, field, sent, outward, base)


def end_kernel(turned, pair, near, far, local, returned, own):
    face = returned.shape[0]
    total = apply_out(turned, pair, near, far, local)
    returned[...] = total[0:face, :].astype(BF16)
    own[...] = total[face:, :]


def last_kernel(own, received, state, first, mass, send, second):
    m = widen(column(mass[...]), state.shape[1])
    owned = own[...] + dot(hot_columns(send[...], state.shape[0]), received[...])
    two = filter_scale * (m * owned - filter_shift * first[...].astype(F32))
    second[...] = (two - state[...].astype(F32)).astype(BF16)


def call(kernel, outs, args, specs=None, scratch=(), mib=8):
    return pl.pallas_call(
        kernel,
        out_shape=[
            kept[0](*kept[1:]) if kept else jax.ShapeDtypeStruct(shape, kind)
            for shape, kind, *kept in outs
        ],
        in_specs=specs or [VMEM] * len(args),
        out_specs=[VMEM] * len(outs),
        scratch_shapes=list(scratch),
        compiler_params=pltpu.CompilerParams(vmem_limit_bytes=mib << 20),
    )(*args)


def kept(shape, kind):
    return (shape, kind, pltpu.VMEM, shape, kind)


def hold(block):
    return pltpu.with_memory_space_constraint(block, pltpu.VMEM)


def leave(block):
    return pltpu.with_memory_space_constraint(block, pltpu.HBM)


def inner_pairs(block):
    n = lax.axis_size("mesh")
    groups = [[i, i + 1] for i in range(0, n, 2)]
    return lax.all_gather(block, "mesh", axis=0, axis_index_groups=groups)


def outer_swap(block):
    n = lax.axis_size("mesh")
    route = [(i, i + 1 if i % 2 else i - 1) for i in range(1, n - 1)]
    return lax.ppermute(block, "mesh", route)


def two_away(block, way):
    n = lax.axis_size("mesh")
    route = [(i, i + (2 * way if i % 2 == 0 else -2 * way)) for i in range(n)]
    return lax.ppermute(block, "mesh", [(i, j) for i, j in route if 0 <= j < n])


def swap(block, axis, mask):
    return lax.ppermute(block, axis, [(i, i ^ mask) for i in range(lax.axis_size(axis))])


def shards(
    state,
    prev_state,
    mass,
    cell_nodes,
    cell_live,
    cell_scale,
    potential,
    stiffness,
    shape_values,
    cell_proj,
    cell_owner,
    cell_slot,
    coupling,
    send_rows,
):
    own_rows, orbitals = state.shape
    cells, per_cell = cell_nodes.shape
    atoms, per_atom = coupling.shape
    face = send_rows.shape[1]
    extended = own_rows + face
    block = atoms * per_atom
    window = 5 * block
    mass_row = mass.reshape(1, own_rows)
    start = call
    scaled, outgoing, strengths, own_proj = start(
        start_kernel,
        [
            ((own_rows, orbitals), BF16),
            ((face + 16, orbitals), BF16),
            ((16, orbitals), BF16),
            (cell_proj.shape, BF16),
        ],
        [leave(block) for block in (state, mass_row, send_rows, coupling, cell_proj)],
    )
    other = swap(cell_proj, "band", 2)
    ghost = from_behind(outgoing, "mesh", 1)

    (pick,) = call(pick_kernel, [kept((cells * per_cell, extended), BF16)], (leave(cell_nodes),))
    pick = hold(pick)
    near = jnp.stack([own_proj, other])
    far = swap(near, "band", 6)
    (operator,) = call(
        operator_kernel,
        [kept((cells, per_cell, per_cell), BF16)],
        (potential, stiffness, shape_values, cell_live, cell_scale),
        specs=[VMEM, VMEM, VMEM, SMEM, SMEM],
    )
    operator = hold(operator)
    projectors = lax.all_gather(
        jnp.concatenate([near, far], axis=0),
        "band",
        axis=0,
        axis_index_groups=[[0, 1], [2, 3], [4, 5], [6, 7]],
    )

    sums_of = [((block, orbitals), BF16), ((2 * block, orbitals), BF16), ((2 * block, orbitals), F32)]
    table, *sums = call(
        table_kernel,
        [kept((window, extended), BF16)] + sums_of,
        (projectors, pick, cell_owner, cell_slot, cell_live, ghost, scaled),
        specs=[VMEM, VMEM, SMEM, SMEM, SMEM, VMEM, VMEM],
        scratch=[
            pltpu.VMEM((window, extended), F32),
            pltpu.VMEM((extended, orbitals), BF16),
            pltpu.VMEM((per_cell, block), BF16),
        ],
    )
    table = hold(table)
    (turned,) = call(turn_kernel, [kept((extended, window), BF16)], (table,))
    turned = hold(turned)
    (place,) = call(place_kernel, [kept((extended, cells * per_cell), BF16)], (cell_nodes,))
    place = hold(place)

    def atom_values(sums, terms):
        sent, outward, base = sums
        far = two_away(sent, 1)
        near = outer_swap(outward)
        mine, message = call(
            join_kernel,
            [((2 * block, orbitals), F32), ((2 * block + 16, orbitals), BF16)],
            (base, near, far, strengths),
        )
        both = inner_pairs(message)
        pair, sent = call(
            couple_kernel,
            [((2 * block, orbitals), BF16), ((block, orbitals), BF16)],
            (mine, both, strengths),
        )
        far = two_away(sent, -1)
        near = outer_swap(pair)
        (local,) = call(scatter_kernel, [((extended, orbitals), F32)], (place, terms))
        return (pair, near, far), local

    def cell_terms(ghost, scaled):
        (terms,) = call(
            gather_kernel,
            [((cells * per_cell, orbitals), BF16)],
            (pick, operator, ghost, scaled),
            scratch=[
                pltpu.VMEM((extended, orbitals), BF16),
                pltpu.VMEM((cells * per_cell, orbitals), BF16),
            ],
        )
        return terms

    nodal = ((own_rows, orbitals), BF16)
    shared = ((face, orbitals), BF16)
    own_wide = ((own_rows, orbitals), F32)

    values, local = atom_values(sums, cell_terms(ghost, scaled))
    returned, own, _, message = call(
        middle_kernel,
        [shared, own_wide, shared, ((2, face, orbitals), BF16)],
        (turned, *values, local, state, prev_state, mass_row, send_rows),
    )
    outer = outer_swap(message[1])
    inner = inner_pairs(message[0])
    first, scaled_one, ghost_one, *sums_one = call(
        next_kernel,
        [nodal, nodal, shared] + sums_of,
        (own, inner, outer, returned, ghost, state, prev_state, mass_row, send_rows, table),
        scratch=[pltpu.VMEM((extended, orbitals), BF16)],
    )
    terms_one = cell_terms(ghost_one, scaled_one)
    values_one, local_one = atom_values(sums_one, terms_one)
    returned_one, own_one = call(
        end_kernel, [shared, own_wide], (turned, *values_one, local_one)
    )
    received_one = from_behind(returned_one, "mesh", -1)
    (second,) = call(
        last_kernel, [nodal], (own_one, received_one, state, first, mass_row, send_rows)
    )
    return (first, second)


def solution(mesh):
    placed = (
        P("mesh", "band"),
        P("mesh", "band"),
        P("mesh"),
        P("mesh", None),
        P("mesh"),
        P("mesh"),
        P("mesh", None),
        P(),
        P(),
        P("mesh", "band", None),
        P("mesh", None),
        P("mesh", None),
        P("mesh", None),
        P("mesh", None),
    )

    return jax.shard_map(
        shards,
        mesh=mesh,
        in_specs=placed,
        out_specs=(P("mesh", "band"), P("mesh", "band")),
        check_vma=False,
    )
```
